32 devices in a mesh: mem: 8 (over y, x, core), lat: 4 (over z).
Axes of the slice: x: 2, y: 2, z: 4, core: 2. Of those that a mesh axis runs over, the one named last changes fastest.
Arguments:
- coarse_weights: bfloat16 [32, 32, 8, 128], P('lat', 'mem'), may hold values from -6 to 6
- perturbations: bfloat16 [32, 8, 128, 512], P('mem', None, 'lat'), may hold values from -6 to 6
- lat_matrix: bfloat16 [128, 32], P('lat'), may hold values from -1 to 1
- lon_matrix: bfloat16 [128, 512], replicated, may hold values from -0.5 to 0.5
- wind_field: float32 [2, 128, 512], P(None, 'lat', 'mem'), may hold values from -0.4 to 0.4
- observed_cell: int32 [4, 8, 128, 64], P(None, None, 'lat', 'mem'), may hold values from 0 to 7
- observed_value: float32 [4, 8, 128, 64], P(None, None, 'lat', 'mem'), may hold values from -6 to 6
- observed_weight: float32 [4, 8, 128, 64], P(None, None, 'lat', 'mem'), may hold values from 0.5 to 4
Outputs:
- gradient: float32 [32, 32, 8, 128], P('lat', 'mem')
- increment: float32 [8, 128, 512], P(None, 'lat', 'mem')
The draws below stay inside these ranges and needn't reach their ends.
Inputs may be any that keep to these rules, and one draw needn't show every extreme that they name: `observed_cell`: the observed cell is an offset within its block of 8 longitudes.
All inputs are finite; a program needn't handle non-finite values.
Results may differ from the reference program's by a relative error of at most 0.0003.
Values may be sent and summed in bfloat16 or wider, within the bound.
A program may use at most 64 MiB of HBM per device.

```python
import math
import jax
import jax.numpy as jnp
from jax import lax

LEV = 8
STEPS = 4
OBLK = 8
MEMBERS = 32
FLAT = 128
FLON = 512
CLAT = 32
CLON = 128


def touch_ends(result, key, smallest, high):
    longest = result.shape.index(max(result.shape))
    spots = []
    for shift in (0, 1):
        where = [jax.random.randint(jax.random.fold_in(key, axis), (), 0, length) for axis, length in enumerate(result.shape)]
        where[longest] = (where[longest] + shift) % result.shape[longest]
        spots.append(tuple(where))
    return result.at[spots[0]].set(smallest).at[spots[1]].set(high)


def block_scale(own_key, shape, pieces, least, largest):
    level = 1.0
    for axis_at, shards_of in pieces:
        steps = jax.random.uniform(jax.random.fold_in(jax.random.fold_in(own_key, 6), axis_at), (shards_of,), jnp.float32, least / len(pieces), largest / len(pieces))
        level = level * jnp.repeat(jnp.exp(steps), shape[axis_at] // shards_of).reshape((-1,) + (1,) * (len(shape) - 1 - axis_at))
    return level


def centred(own_key, dims, width, limit, pieces=(), kind=jnp.bfloat16):
    drawn = width * jax.random.normal(own_key, dims, jnp.float32)
    if pieces:
        drawn = drawn * block_scale(own_key, dims, pieces, -0.22, 0.18)
    return jnp.clip(drawn, -limit, limit).astype(kind)


def setup_inputs(seed: int = 0) -> dict:
    arg_keys = jax.random.split(jax.random.key(seed), 9)
    coarse_weights = centred(arg_keys[0], (CLAT, MEMBERS, LEV, CLON), 1.0, 6.0, ((0, 4), (1, 8)))
    perturbations = centred(arg_keys[1], (MEMBERS, LEV, FLAT, FLON), 1.0, 6.0, ((0, 8), (2, 4)))
    lat_matrix = centred(arg_keys[2], (FLAT, CLAT), CLAT ** -0.5, 1.0, ((0, 4),))
    lon_matrix = centred(arg_keys[3], (CLON, FLON), CLON ** -0.5, 0.5)
    wind_field = jnp.clip(jax.random.uniform(arg_keys[4], (2, FLAT, FLON), jnp.float32, -0.4, 0.4) * block_scale(arg_keys[4], (2, FLAT, FLON), ((1, 4), (2, 8)), -0.4, 0.0), -0.4, 0.4)
    observed_cell = touch_ends(jax.random.randint(arg_keys[5], (STEPS, LEV, FLAT, FLON // OBLK), 0, OBLK), jax.random.fold_in(arg_keys[5], 1), 0, OBLK - 1).astype(jnp.int32)
    observed_value = centred(arg_keys[6], (STEPS, LEV, FLAT, FLON // OBLK), 1.0, 6.0, ((2, 4), (3, 8)), jnp.float32)
    observed_weight = jnp.clip(jnp.exp(math.log(4.0) - 2.0794415 * jax.random.uniform(arg_keys[7], (STEPS, LEV, FLAT, FLON // OBLK), jnp.float32) ** block_scale(arg_keys[7], (STEPS, LEV, FLAT, FLON // OBLK), ((2, 4), (3, 8)), -0.2, 0.2)), 0.5, 4.0)
    return dict(coarse_weights=coarse_weights, perturbations=perturbations, lat_matrix=lat_matrix, lon_matrix=lon_matrix, wind_field=wind_field, observed_cell=observed_cell, observed_value=observed_value, observed_weight=observed_weight)


diffusion = 0.2
highest = lax.Precision.HIGHEST

def stencil_parts(padded):
    center = padded[:, 1:-1, 1:-1]
    north_cell = padded[:, 2:, 1:-1]
    south_cell = padded[:, :-2, 1:-1]
    east_cell = padded[:, 1:-1, 2:]
    west_cell = padded[:, 1:-1, :-2]
    return (center, north_cell, south_cell, east_cell, west_cell)

def advance(padded, wind_out):
    center, north_cell, south_cell, east_cell, west_cell = stencil_parts(padded)
    spread = north_cell + south_cell + east_cell + west_cell - 4.0 * center
    return center + diffusion * spread - 0.5 * wind_out[1] * (north_cell - south_cell) - 0.5 * wind_out[0] * (east_cell - west_cell)

def retreat(padded, wind_in):
    center, north_cell, south_cell, east_cell, west_cell = stencil_parts(padded)
    spread = north_cell + south_cell + east_cell + west_cell - 4.0 * center
    along_lon = wind_in[0] * padded
    along_lat = wind_in[1] * padded
    return center + diffusion * spread + 0.5 * (along_lat[:, 2:, 1:-1] - along_lat[:, :-2, 1:-1]) + 0.5 * (along_lon[:, 1:-1, 2:] - along_lon[:, 1:-1, :-2])

def observe(tangent, picked, observed, weighting):
    levels, row_count, col_count = tangent.shape
    blocks = tangent.reshape(levels, row_count, col_count // OBLK, OBLK)
    onehot = (picked[..., None] == jnp.arange(OBLK, dtype=jnp.int32)).astype(jnp.float32)
    looked = lax.optimization_barrier(jnp.sum(blocks * onehot, axis=-1))
    misfit = weighting * (looked - observed)
    return (misfit[..., None] * onehot).reshape(levels, row_count, col_count)

def reference(coarse_weights, perturbations, lat_matrix, lon_matrix, wind_field, observed_cell, observed_value, observed_weight):
    member_scale = 1.0 / jnp.sqrt(jnp.float32(MEMBERS - 1))
    lat_full = lat_matrix.astype(jnp.float32)
    lon_full = lon_matrix.astype(jnp.float32)
    by_member = jnp.transpose(coarse_weights, (1, 0, 2, 3))

    def member_term(running, inputs):
        coarse, member = inputs
        partly = jnp.einsum('rc,clw->lrw', lat_full, coarse.astype(jnp.float32), precision=highest)
        localized = jnp.einsum('lrw,wf->lrf', partly, lon_full, precision=highest)
        return (running + localized * member.astype(jnp.float32), None)
    summed, _ = lax.scan(member_term, jnp.zeros((LEV, FLAT, FLON), jnp.float32), (by_member, perturbations))
    increment = summed * member_scale
    margin_one = ((0, 0), (1, 1), (1, 1))
    wind_padded = jnp.pad(wind_field, margin_one)
    tangent = increment
    forcings = []
    for step_index in range(STEPS):
        tangent = advance(jnp.pad(tangent, margin_one), wind_field)
        forcings.append(observe(tangent, observed_cell[step_index], observed_value[step_index], observed_weight[step_index]))
    adjoint = jnp.zeros_like(increment)
    for step_index in reversed(range(STEPS)):
        adjoint = retreat(jnp.pad(adjoint + forcings[step_index], margin_one), wind_padded)

    def member_grad(unused, inputs):
        coarse, member = inputs
        product = member.astype(jnp.float32) * adjoint
        partly = jnp.einsum('lrf,wf->lrw', product, lon_full, precision=highest)
        gradient = jnp.einsum('rc,lrw->clw', lat_full, partly, precision=highest)
        return (unused, gradient * member_scale + coarse.astype(jnp.float32))
    _, grads = lax.scan(member_grad, jnp.float32(0.0), (by_member, perturbations))
    return (jnp.transpose(grads, (1, 0, 2, 3)), increment)
```

```python
import functools

import jax
import jax.numpy as jnp
from jax import lax
from jax.experimental import pallas as pl
from jax.experimental.pallas import tpu as pltpu
from jax.sharding import PartitionSpec as P

STEPS = 4
OBLK = 8
HALO = 2 * STEPS
LANES = 128
DIFFUSION = 0.2
F32 = jnp.float32
BF16 = jnp.bfloat16


def split2(x):
    hi = x.astype(BF16)
    return hi, (x - hi.astype(F32)).astype(BF16)


def dot(a, b, dims=((1,), (0,))):
    return lax.dot_general(a, b, (dims, ((), ())), preferred_element_type=F32)


def kernel(
    nmem,
    nlat,
    scale,
    coarse_ref,
    pert_ref,
    lat_ref,
    lon_ref,
    aux_ref,
    band_ref,
    inc_ref,
    cg,
    auxg,
    part,
    pr,
    rs,
    ext,
    spread,
    coef,
    wts,
    vals,
    itile,
    incr,
    adjg,
    gb,
    gr,
    cg_ss,
    cg_rs,
    aux_ss,
    aux_rs,
    ah_ss,
    ah_rs,
    pr_ss,
    pr_rs,
    rs_ss,
    rs_rs,
    halo_ss,
    halo_rs,
    inc_ss,
    inc_rs,
    adj_ss,
    adj_rs,
    rel_ss,
    rel_rs,
    g_ss,
    g_rs,
):
    members, lev, rows, flon = pert_ref.shape
    clon = lon_ref.shape[0]
    cols = flon // nmem
    groups = nmem // lev
    urows = rows // groups
    erows = urows + 2 * HALO
    npairs = nmem // 2
    me = lax.axis_index("mem")
    z = lax.axis_index("lat")
    pair = me // 2
    core = me % 2
    partner = pair * 2 + (1 - core)
    my_level = me // groups
    my_group = me % groups
    my_row = my_group * urows
    block = z * groups + my_group
    has_up = block > 0
    has_down = block < nlat * groups - 1

    def neighbour(shift):
        there = block + shift
        return (my_level * groups + (there + groups) % groups, (there + groups) // groups - 1)

    up = neighbour(-1)
    down = neighbour(1)

    def send(src, dst, ss, rsem, mem, lat):
        return pltpu.make_async_remote_copy(
            src_ref=src,
            dst_ref=dst,
            send_sem=ss,
            recv_sem=rsem,
            device_id={"mem": mem, "lat": lat},
            device_id_type=pl.DeviceIdType.MESH,
        )

    barrier = pltpu.get_barrier_semaphore()

    def greet(mem, lat):
        pl.semaphore_signal(
            barrier, inc=1, device_id={"mem": mem, "lat": lat}, device_id_type=pl.DeviceIdType.MESH
        )

    for i in range(1, nmem):
        greet((me + i) % nmem, z)
    for i in range(1, nlat):
        greet(me, (z + i) % nlat)
    pl.semaphore_wait(barrier, nmem + nlat - 2)
    if groups > 1:
        far_up = has_up & (my_group == 0)
        far_down = has_down & (my_group == groups - 1)

        @pl.when(far_up)
        def _():
            greet(*up)

        @pl.when(far_down)
        def _():
            greet(*down)

        @pl.when(far_up)
        def _():
            pl.semaphore_wait(barrier, 1)

        @pl.when(far_down)
        def _():
            pl.semaphore_wait(barrier, 1)

    def cg_copy(there):
        return send(coarse_ref, cg.at[z], cg_ss.at[there], cg_rs.at[z], me, there)

    def cg_arrival(source):
        return send(coarse_ref, cg.at[source], cg_ss.at[source], cg_rs.at[source], me, source)

    for i in range(1, nlat):
        cg_copy((z + i) % nlat).start()

    def aux_copy(there):
        return send(
            aux_ref.at[there // groups, pl.ds(pl.multiple_of((there % groups) * urows, 8), urows)],
            auxg.at[me, pl.ds(HALO, urows)],
            aux_ss.at[there],
            aux_rs.at[me],
            there,
            z,
        )

    def aux_arrival(source):
        return send(
            aux_ref.at[0, pl.ds(0, urows)],
            auxg.at[source, pl.ds(HALO, urows)],
            aux_ss.at[source],
            aux_rs.at[source],
            source,
            z,
        )

    for i in range(1, nmem):
        aux_copy((me + i) % nmem).start()

    cg[z] = coarse_ref[...]
    auxg[me, HALO : HALO + urows] = aux_ref[my_level, pl.ds(pl.multiple_of(my_row, 8), urows)]

    @pl.when(jnp.logical_not(has_up))
    def _():
        auxg[:, :HALO] = jnp.zeros((nmem, HALO, 2 * LANES), F32)
        ext[:HALO] = jnp.zeros((HALO, flon), F32)

    @pl.when(jnp.logical_not(has_down))
    def _():
        auxg[:, HALO + urows :] = jnp.zeros((nmem, HALO, 2 * LANES), F32)
        ext[HALO + urows :] = jnp.zeros((HALO, flon), F32)

    per_tile = cols // OBLK
    k = lax.broadcasted_iota(jnp.int32, (2 * LANES, LANES), 0)
    n = lax.broadcasted_iota(jnp.int32, (2 * LANES, LANES), 1)
    for piece in range(3 * STEPS):
        hit = k == (n // cols) * LANES + piece * per_tile + (n % cols) // OBLK
        spread[:, piece * LANES : (piece + 1) * LANES] = jnp.where(hit, 1.0, 0.0).astype(BF16)

    lat_f32 = lat_ref[...].astype(F32)
    lat_bf = lat_ref[...]
    lat_t = jnp.transpose(lat_f32).astype(BF16)
    lat_t2 = jnp.concatenate([lat_t, lat_t], axis=1)
    lon = lon_ref[...]

    for i in range(1, nlat):
        cg_arrival((z + nlat - i) % nlat).wait_recv()

    def pr_copy(p):
        unit = 2 * p + (1 - core)
        return send(part.at[unit], pr.at[p], pr_ss.at[p], pr_rs.at[p], partner, z)

    def pr_arrival(p):
        return send(part.at[2 * p + core], pr.at[p], pr_ss.at[p], pr_rs.at[p], partner, z)

    def forward(i, carry):
        if groups == 1:
            half = lev // 2
            level = jnp.where(i < half, 2 * i + (1 - core), 2 * (i - half) + core)
        else:
            level = i
        coarse = jnp.concatenate(
            [cg[:, m, level].astype(F32).reshape(-1, clon) for m in range(members)], axis=1
        ).astype(BF16)
        partly = dot(lat_bf, coarse)
        partly = jnp.concatenate(
            [partly[:, m * clon : (m + 1) * clon] for m in range(members)], axis=0
        )
        hi, lo = split2(partly)
        localized = dot(hi, lon) + dot(lo, lon)
        total = localized[:rows] * pert_ref[0, level].astype(F32)
        for m in range(1, members):
            total += localized[m * rows : (m + 1) * rows] * pert_ref[m, level].astype(F32)
        part[pl.ds(level * groups, groups)] = total.reshape(groups, urows, flon)
        if groups == 1:

            @pl.when(i < lev // 2)
            def _():
                pr_copy(i).start()

        else:
            for g in range(groups // 2):
                pr_copy(level * (groups // 2) + g).start()
        return carry

    lax.fori_loop(0, lev, forward, 0)

    for i in range(1, nmem):
        aux_arrival((me + nmem - i) % nmem).wait_recv()
    ah_up = send(
        auxg.at[:, pl.ds(HALO, HALO)],
        auxg.at[:, pl.ds(HALO + urows, HALO)],
        ah_ss.at[0],
        ah_rs.at[0],
        *up,
    )
    ah_down = send(
        auxg.at[:, pl.ds(urows, HALO)], auxg.at[:, pl.ds(0, HALO)], ah_ss.at[1], ah_rs.at[1], *down
    )

    @pl.when(has_up)
    def _():
        ah_up.start()

    @pl.when(has_down)
    def _():
        ah_down.start()

    def rs_copy(p):
        return send(pr.at[p], rs.at[pair], rs_ss.at[p], rs_rs.at[pair], 2 * p + core, z)

    def rs_arrival(p):
        return send(pr.at[p], rs.at[p], rs_ss.at[p], rs_rs.at[p], 2 * p + core, z)

    def combine(i, carry):
        p = (pair + 1 + i) % npairs
        pr_arrival(p).wait_recv()
        pr[p] = pr[p] + part[2 * p + core]

        @pl.when(p != pair)
        def _():
            rs_copy(p).start()

        return carry

    lax.fori_loop(0, npairs, combine, 0)

    @pl.when(has_down)
    def _():
        ah_up_arrival = send(
            auxg.at[:, pl.ds(HALO, HALO)],
            auxg.at[:, pl.ds(HALO + urows, HALO)],
            ah_ss.at[0],
            ah_rs.at[0],
            *down,
        )
        ah_up_arrival.wait_recv()

    @pl.when(has_up)
    def _():
        ah_down_arrival = send(
            auxg.at[:, pl.ds(urows, HALO)],
            auxg.at[:, pl.ds(0, HALO)],
            ah_ss.at[1],
            ah_rs.at[1],
            *up,
        )
        ah_down_arrival.wait_recv()

    @pl.when(has_up)
    def _():
        ah_up.wait_send()

    @pl.when(has_down)
    def _():
        ah_down.wait_send()

    place = block * urows - HALO + lax.broadcasted_iota(jnp.int32, (erows, LANES), 0)
    inside = (place >= 0) & (place < nlat * rows)
    lane = lax.broadcasted_iota(jnp.int32, (erows, LANES), 1)
    tiles = LANES // cols
    for q in range(flon // LANES):
        first, second = auxg[tiles * q], auxg[tiles * q + 1]
        lhs = jnp.concatenate([first[:, :LANES], second[:, :LANES]], axis=1)
        hi, rest = lhs.astype(BF16), lhs
        rest = rest - hi.astype(F32)
        mid, low = split2(rest)
        out = dot(jnp.concatenate([hi, mid, low], axis=0), spread[...])
        out = out[:erows] + out[erows : 2 * erows] + out[2 * erows :]
        at = slice(q * LANES, (q + 1) * LANES)
        for t in range(STEPS):
            weight = out[:, t * LANES : (t + 1) * LANES]
            value = out[:, (STEPS + t) * LANES : (STEPS + t + 1) * LANES]
            cell = out[:, (2 * STEPS + t) * LANES : (2 * STEPS + t + 1) * LANES]
            hit = cell == (lane % OBLK).astype(F32)
            wts[t, :, at] = jnp.where(hit, weight, 0.0)
            vals[t, :, at] = value
        w0, w1 = first[:, LANES:], second[:, LANES:]
        lower = lane < cols
        c0 = jnp.where(lower, w0, pltpu.roll(w1, cols, 1))
        c1 = jnp.where(lower, pltpu.roll(w0, cols, 1), w1)
        east_in = inside & (lane + q * LANES < flon - 1)
        west_in = inside & (lane + q * LANES > 0)
        coef[0, :, at] = jnp.where(inside, DIFFUSION - 0.5 * c1, 0.0)
        coef[1, :, at] = jnp.where(inside, DIFFUSION + 0.5 * c1, 0.0)
        coef[2, :, at] = jnp.where(east_in, DIFFUSION - 0.5 * c0, 0.0)
        coef[3, :, at] = jnp.where(west_in, DIFFUSION + 0.5 * c0, 0.0)
        coef[4, :, at] = jnp.where(inside, jnp.full((erows, LANES), 1.0 - 4.0 * DIFFUSION, F32), 0.0)

    total = pr[pair]
    for i in range(1, npairs):
        p = (pair + npairs - i) % npairs
        rs_arrival(p).wait_recv()
        total = total + rs[p]
    total = total * scale
    ext[HALO : HALO + urows] = total
    halo_up = send(
        ext.at[pl.ds(HALO, HALO)],
        ext.at[pl.ds(HALO + urows, HALO)],
        halo_ss.at[0],
        halo_rs.at[0],
        *up,
    )
    halo_down = send(
        ext.at[pl.ds(urows, HALO)], ext.at[pl.ds(0, HALO)], halo_ss.at[1], halo_rs.at[1], *down
    )

    @pl.when(has_up)
    def _():
        halo_up.start()

    @pl.when(has_down)
    def _():
        halo_down.start()

    for m in range(nmem):
        itile[m] = total[:, m * cols : (m + 1) * cols]

    def inc_copy(there):
        return send(
            itile.at[there],
            incr.at[my_level, pl.ds(pl.multiple_of(my_row, 8), urows)],
            inc_ss.at[there],
            inc_rs.at[me],
            there,
            z,
        )

    def inc_arrival(source):
        return send(
            itile.at[source],
            incr.at[
                source // groups, pl.ds(pl.multiple_of((source % groups) * urows, 8), urows)
            ],
            inc_ss.at[source],
            inc_rs.at[source],
            source,
            z,
        )

    for i in range(1, nmem):
        inc_copy((me + i) % nmem).start()
    incr[my_level, pl.ds(pl.multiple_of(my_row, 8), urows)] = itile[me]

    @pl.when(has_down)
    def _():
        send(
            ext.at[pl.ds(HALO, HALO)],
            ext.at[pl.ds(HALO + urows, HALO)],
            halo_ss.at[0],
            halo_rs.at[0],
            *down,
        ).wait_recv()

    @pl.when(has_up)
    def _():
        send(
            ext.at[pl.ds(urows, HALO)], ext.at[pl.ds(0, HALO)], halo_ss.at[1], halo_rs.at[1], *up
        ).wait_recv()

    @pl.when(has_up)
    def _():
        halo_up.wait_send()

    @pl.when(has_down)
    def _():
        halo_down.wait_send()

    state = ext[...]
    forcing = []
    for t in range(STEPS):
        state = (
            coef[4] * state
            + coef[0] * pltpu.roll(state, erows - 1, 0)
            + coef[1] * pltpu.roll(state, 1, 0)
            + coef[2] * pltpu.roll(state, flon - 1, 1)
            + coef[3] * pltpu.roll(state, 1, 1)
        )
        wts[t] = wts[t] * (state - vals[t])
    adjoint = None
    for t in reversed(range(STEPS)):
        adjoint = wts[t] if adjoint is None else adjoint + wts[t]
        adjoint = (
            coef[4] * adjoint
            + pltpu.roll(coef[1] * adjoint, erows - 1, 0)
            + pltpu.roll(coef[0] * adjoint, 1, 0)
            + pltpu.roll(coef[3] * adjoint, flon - 1, 1)
            + pltpu.roll(coef[2] * adjoint, 1, 1)
        )
    adjg[me] = adjoint[HALO : HALO + urows]

    def adj_copy(p):
        return send(adjg.at[me], adjg.at[me], adj_ss.at[p], adj_rs.at[pair], 2 * p + core, z)

    def adj_arrival(p):
        unit = 2 * p + core
        return send(adjg.at[unit], adjg.at[unit], adj_ss.at[p], adj_rs.at[p], unit, z)

    def relay(p):
        unit = 2 * p + core
        return send(adjg.at[unit], adjg.at[unit], rel_ss.at[p], rel_rs.at[p], partner, z)

    def relay_arrival(p):
        unit = 2 * p + (1 - core)
        return send(adjg.at[unit], adjg.at[unit], rel_ss.at[p], rel_rs.at[p], partner, z)

    for i in range(1, npairs):
        adj_copy((pair + i) % npairs).start()

    def g_copy(there, level):
        return send(
            gb.at[there, level], gr.at[z, level], g_ss.at[there, level], g_rs.at[z, level], me, there
        )

    def g_arrival(source, level):
        return send(
            gb.at[source, level],
            gr.at[source, level],
            g_ss.at[source, level],
            g_rs.at[source, level],
            me,
            source,
        )

    def backward(level):
        field = adjg[pl.ds(level * groups, groups)].reshape(rows, flon)
        product = jnp.concatenate(
            [pert_ref[m, level].astype(F32) * field for m in range(members)], axis=0
        )
        hi, lo = split2(product)
        over_lon = ((1,), (1,))
        projected = dot(hi, lon, over_lon) + dot(lo, lon, over_lon)
        projected = jnp.concatenate(
            [projected[m * rows : (m + 1) * rows] for m in range(members)], axis=1
        )
        hi, lo = split2(projected)
        banded = dot(lat_t2, jnp.concatenate([hi, lo], axis=0))
        gb[:, level] = banded.reshape(nlat, -1, members * clon)
        for i in range(1, nlat):
            g_copy((z + i) % nlat, level).start()

    def near(i, carry):
        p = (pair + npairs - i) % npairs

        @pl.when(i > 0)
        def _():
            adj_arrival(p).wait_recv()

        relay(p).start()
        if groups == 1:
            backward(2 * p + core)
        return carry

    lax.fori_loop(0, npairs, near, 0)

    def far(i, carry):
        p = (pair + npairs - i) % npairs
        relay_arrival(p).wait_recv()
        if groups == 1:
            backward(2 * p + (1 - core))
        elif groups == 2:
            backward(p)
        else:

            @pl.when(p % (groups // 2) == groups // 2 - 1)
            def _():
                backward(p // (groups // 2))

        return carry

    lax.fori_loop(0, npairs, far, 0)

    for i in range(1, nmem):
        inc_arrival((me + nmem - i) % nmem).wait_recv()
    inc_ref[...] = incr[...]

    def finish(level, carry):
        total = gb[z, level]
        for i in range(1, nlat):
            source = (z + nlat - i) % nlat
            g_arrival(source, level).wait_recv()
            total = total + gr[source, level]
        band_ref[level] = total
        return carry

    lax.fori_loop(0, lev, finish, 0)

    for i in range(1, nlat):
        cg_copy((z + i) % nlat).wait_send()
    for i in range(1, nmem):
        aux_copy((me + i) % nmem).wait_send()
        inc_copy((me + i) % nmem).wait_send()
    for p in range(npairs):
        pr_copy(p).wait_send()
        relay(p).wait_send()
    for i in range(1, npairs):
        rs_copy((pair + i) % npairs).wait_send()
        adj_copy((pair + i) % npairs).wait_send()

    def drain(level, carry):
        for i in range(1, nlat):
            g_copy((z + i) % nlat, level).wait_send()
        return carry

    lax.fori_loop(0, lev, drain, 0)


def body(
    nmem,
    nlat,
    coarse_weights,
    perturbations,
    lat_matrix,
    lon_matrix,
    wind_field,
    observed_cell,
    observed_value,
    observed_weight,
):
    members, lev, rows, flon = perturbations.shape
    cband, _, _, clon = coarse_weights.shape
    cols = wind_field.shape[2]
    blocks = cols // OBLK
    groups = nmem // lev
    urows = rows // groups
    erows = urows + 2 * HALO
    npairs = nmem // 2
    assert nmem == lev * groups and nmem % 2 == 0 and urows % 8 == 0 and urows >= HALO
    assert 2 * cols == LANES and 3 * STEPS * blocks <= LANES
    scale = 1.0 / jnp.sqrt(jnp.float32(members * nmem - 1))
    coarse_t = jnp.transpose(coarse_weights, (1, 2, 0, 3))
    obs = jnp.stack([observed_weight, observed_value, observed_cell.astype(F32)])
    obs = jnp.transpose(obs, (2, 3, 0, 1, 4)).reshape(lev, rows, 3 * STEPS * blocks)
    obs = jnp.pad(obs, ((0, 0), (0, 0), (0, LANES - obs.shape[2])))
    wind = jnp.transpose(wind_field, (1, 0, 2)).reshape(1, rows, 2 * cols)
    aux = jnp.concatenate([obs, jnp.broadcast_to(wind, (lev, rows, LANES))], axis=2)
    vmem = pl.BlockSpec(memory_space=pltpu.VMEM)
    dma = pltpu.SemaphoreType.DMA
    width = members * clon
    banded, increment = pl.pallas_call(
        functools.partial(kernel, nmem, nlat, float(1.0 / (members * nmem - 1) ** 0.5)),
        out_shape=(
            jax.ShapeDtypeStruct((lev, cband, width), F32),
            jax.ShapeDtypeStruct((lev, rows, cols), F32),
        ),
        in_specs=[vmem] * 5,
        out_specs=(vmem, vmem),
        scratch_shapes=[
            pltpu.VMEM((nlat, members, lev, cband, clon), BF16),
            pltpu.VMEM((nmem, erows, 2 * LANES), F32),
            pltpu.VMEM((nmem, urows, flon), F32),
            pltpu.VMEM((npairs, urows, flon), F32),
            pltpu.VMEM((npairs, urows, flon), F32),
            pltpu.VMEM((erows, flon), F32),
            pltpu.VMEM((2 * LANES, 3 * STEPS * LANES), BF16),
            pltpu.VMEM((5, erows, flon), F32),
            pltpu.VMEM((STEPS, erows, flon), F32),
            pltpu.VMEM((STEPS, erows, flon), F32),
            pltpu.VMEM((nmem, urows, cols), F32),
            pltpu.VMEM((lev, rows, cols), F32),
            pltpu.VMEM((nmem, urows, flon), F32),
            pltpu.VMEM((nlat, lev, cband, width), F32),
            pltpu.VMEM((nlat, lev, cband, width), F32),
            dma((nlat,)),
            dma((nlat,)),
            dma((nmem,)),
            dma((nmem,)),
            dma((2,)),
            dma((2,)),
            dma((npairs,)),
            dma((npairs,)),
            dma((npairs,)),
            dma((npairs,)),
            dma((2,)),
            dma((2,)),
            dma((nmem,)),
            dma((nmem,)),
            dma((npairs,)),
            dma((npairs,)),
            dma((npairs,)),
            dma((npairs,)),
            dma((nlat, lev)),
            dma((nlat, lev)),
        ],
        compiler_params=pltpu.CompilerParams(
            collective_id=0, has_side_effects=True, vmem_limit_bytes=60 * 1024 * 1024
        ),
    )(coarse_t, perturbations, lat_matrix, lon_matrix, aux)
    banded = jnp.transpose(banded.reshape(lev, cband, members, clon), (1, 2, 0, 3))
    return banded * scale + coarse_weights.astype(F32), increment


def solution(mesh):
    in_specs = (
        P("lat", "mem", None, None),
        P("mem", None, "lat", None),
        P("lat", None),
        P(),
        P(None, "lat", "mem"),
        P(None, None, "lat", "mem"),
        P(None, None, "lat", "mem"),
        P(None, None, "lat", "mem"),
    )
    out_specs = (P("lat", "mem", None, None), P(None, "lat", "mem"))
    call = functools.partial(body, mesh.shape["mem"], mesh.shape["lat"])
    return jax.shard_map(call, mesh=mesh, in_specs=in_specs, out_specs=out_specs, check_vma=False)
```

```python
import functools

import jax
import jax.numpy as jnp
from jax import lax
from jax.experimental import pallas as pl
from jax.experimental.pallas import tpu as pltpu
from jax.sharding import PartitionSpec as P

STEPS = 4
OBLK = 8
HALO = 2 * STEPS
LANES = 128
DIFFUSION = 0.2
F32 = jnp.float32
BF16 = jnp.bfloat16


def split2(x):
    hi = x.astype(BF16)
    return hi, (x - hi.astype(F32)).astype(BF16)


def dot(a, b, dims=((1,), (0,))):
    return lax.dot_general(a, b, (dims, ((), ())), preferred_element_type=F32)


def kernel(
    nmem,
    nlat,
    scale,
    coarse_hbm,
    pert_hbm,
    lat_hbm,
    lon_hbm,
    wind_hbm,
    cell_hbm,
    value_hbm,
    weight_hbm,
    grad_ref,
    inc_ref,
    coarse_ref,
    pert_ref,
    lat_ref,
    lon_ref,
    wind_ref,
    cell_ref,
    value_ref,
    weight_ref,
    aux_ref,
    cg,
    auxg,
    part,
    pr,
    rs,
    ext,
    spread,
    coef,
    wts,
    vals,
    itile,
    incr,
    adjg,
    gb,
    gr,
    in_sem,
    cg_ss,
    cg_rs,
    aux_ss,
    aux_rs,
    ah_ss,
    ah_rs,
    pr_ss,
    pr_rs,
    rs_ss,
    rs_rs,
    halo_ss,
    halo_rs,
    inc_ss,
    inc_rs,
    adj_ss,
    adj_rs,
    rel_ss,
    rel_rs,
    g_ss,
    g_rs,
):
    members, lev, rows, flon = pert_ref.shape
    clon = lon_ref.shape[0]
    cols = flon // nmem
    groups = nmem // lev
    urows = rows // groups
    erows = urows + 2 * HALO
    npairs = nmem // 2
    me = lax.axis_index("mem")
    z = lax.axis_index("lat")
    pair = me // 2
    core = me % 2
    partner = pair * 2 + (1 - core)
    my_level = me // groups
    my_group = me % groups
    my_row = my_group * urows
    block = z * groups + my_group
    has_up = block > 0
    has_down = block < nlat * groups - 1

    def neighbour(shift):
        there = block + shift
        return (my_level * groups + (there + groups) % groups, (there + groups) // groups - 1)

    up = neighbour(-1)
    down = neighbour(1)

    def send(src, dst, ss, rsem, mem, lat):
        return pltpu.make_async_remote_copy(
            src_ref=src,
            dst_ref=dst,
            send_sem=ss,
            recv_sem=rsem,
            device_id={"mem": mem, "lat": lat},
            device_id_type=pl.DeviceIdType.MESH,
        )

    arguments = (
        (coarse_hbm, coarse_ref),
        (lat_hbm, lat_ref),
        (lon_hbm, lon_ref),
        (wind_hbm, wind_ref),
        (cell_hbm, cell_ref),
        (value_hbm, value_ref),
        (weight_hbm, weight_ref),
        (pert_hbm, pert_ref),
    )
    loads = [
        pltpu.make_async_copy(src, dst, in_sem.at[i]) for i, (src, dst) in enumerate(arguments)
    ]
    for load in loads:
        load.start()

    barrier = pltpu.get_barrier_semaphore()

    def greet(mem, lat):
        pl.semaphore_signal(
            barrier, inc=1, device_id={"mem": mem, "lat": lat}, device_id_type=pl.DeviceIdType.MESH
        )

    for i in range(1, nlat):
        greet(me, (z + i) % nlat)
    for i in range(1, nmem):
        greet((me + i) % nmem, z)
    loads[0].wait()
    for m in range(members):
        mine = jnp.swapaxes(coarse_ref[:, m].astype(F32), 0, 1).astype(BF16)
        for level in range(lev):
            cg[z, level, m] = mine[level]
    pl.semaphore_wait(barrier, nmem + nlat - 2)
    if groups > 1:
        far_up = has_up & (my_group == 0)
        far_down = has_down & (my_group == groups - 1)

        @pl.when(far_up)
        def _():
            greet(*up)

        @pl.when(far_down)
        def _():
            greet(*down)

        @pl.when(far_up)
        def _():
            pl.semaphore_wait(barrier, 1)

        @pl.when(far_down)
        def _():
            pl.semaphore_wait(barrier, 1)

    def level_at(i):
        if groups > 1:
            return i
        half = lev // 2
        p = (pair + 1 + i) % npairs
        return 2 * p + jnp.where(i < half, 1 - core, core)

    def cg_copy(there, level):
        return send(
            cg.at[z, level], cg.at[z, level], cg_ss.at[there, level], cg_rs.at[z, level], me, there
        )

    def cg_arrival(source, level):
        return send(
            cg.at[source, level],
            cg.at[source, level],
            cg_ss.at[source, level],
            cg_rs.at[source, level],
            me,
            source,
        )

    def spread_coarse(i, carry):
        for j in range(1, nlat):
            cg_copy((z + j) % nlat, level_at(i)).start()
        return carry

    lax.fori_loop(0, lev, spread_coarse, 0)

    for load in loads[1:-1]:
        load.wait()

    blank = jnp.zeros((rows, LANES - 3 * STEPS * (cols // OBLK)), F32)
    winds = jnp.concatenate([wind_ref[0], wind_ref[1]], axis=1)

    def pack(level, carry):
        pieces = [ref[t, level] for ref in (weight_ref, value_ref) for t in range(STEPS)]
        pieces += [cell_ref[t, level].astype(F32) for t in range(STEPS)]
        aux_ref[level, :, :LANES] = jnp.concatenate(pieces + [blank], axis=1)
        aux_ref[level, :, LANES:] = winds
        return carry

    lax.fori_loop(0, lev, pack, 0)

    def aux_copy(there):
        return send(
            aux_ref.at[there // groups, pl.ds(pl.multiple_of((there % groups) * urows, 8), urows)],
            auxg.at[me, pl.ds(HALO, urows)],
            aux_ss.at[there],
            aux_rs.at[me],
            there,
            z,
        )

    def aux_arrival(source):
        return send(
            aux_ref.at[0, pl.ds(0, urows)],
            auxg.at[source, pl.ds(HALO, urows)],
            aux_ss.at[source],
            aux_rs.at[source],
            source,
            z,
        )

    for i in range(1, nmem):
        aux_copy((me + i) % nmem).start()

    auxg[me, HALO : HALO + urows] = aux_ref[my_level, pl.ds(pl.multiple_of(my_row, 8), urows)]

    @pl.when(jnp.logical_not(has_up))
    def _():
        auxg[:, :HALO] = jnp.zeros((nmem, HALO, 2 * LANES), F32)
        ext[:HALO] = jnp.zeros((HALO, flon), F32)

    @pl.when(jnp.logical_not(has_down))
    def _():
        auxg[:, HALO + urows :] = jnp.zeros((nmem, HALO, 2 * LANES), F32)
        ext[HALO + urows :] = jnp.zeros((HALO, flon), F32)

    per_tile = cols // OBLK
    k = lax.broadcasted_iota(jnp.int32, (2 * LANES, LANES), 0)
    n = lax.broadcasted_iota(jnp.int32, (2 * LANES, LANES), 1)
    for piece in range(3 * STEPS):
        hit = k == (n // cols) * LANES + piece * per_tile + (n % cols) // OBLK
        spread[:, piece * LANES : (piece + 1) * LANES] = jnp.where(hit, 1.0, 0.0).astype(BF16)

    lat_f32 = lat_ref[...].astype(F32)
    lat_bf = lat_ref[...]
    lat_t = jnp.transpose(lat_f32).astype(BF16)
    lat_t2 = jnp.concatenate([lat_t, lat_t], axis=1)
    lon = lon_ref[...]

    loads[-1].wait()

    def pr_copy(p):
        unit = 2 * p + (1 - core)
        return send(part.at[unit], pr.at[p], pr_ss.at[p], pr_rs.at[p], partner, z)

    def pr_arrival(p):
        return send(part.at[2 * p + core], pr.at[p], pr_ss.at[p], pr_rs.at[p], partner, z)

    def rs_copy(p):
        return send(pr.at[p], rs.at[pair], rs_ss.at[p], rs_rs.at[pair], 2 * p + core, z)

    def rs_arrival(p):
        return send(pr.at[p], rs.at[p], rs_ss.at[p], rs_rs.at[p], 2 * p + core, z)

    def combine(i, carry):
        p = (pair + 1 + i) % npairs
        pr_arrival(p).wait_recv()
        pr[p] = pr[p] + part[2 * p + core]

        @pl.when(p != pair)
        def _():
            rs_copy(p).start()

        return carry

    def forward(i, carry):
        level = level_at(i)
        for j in range(1, nlat):
            cg_arrival((z + nlat - j) % nlat, level).wait_recv()
        coarse = jnp.concatenate(
            [cg[:, level, m].astype(F32).reshape(-1, clon) for m in range(members)], axis=1
        ).astype(BF16)
        partly = dot(lat_bf, coarse)
        partly = jnp.concatenate(
            [partly[:, m * clon : (m + 1) * clon] for m in range(members)], axis=0
        )
        hi, lo = split2(partly)
        localized = dot(hi, lon) + dot(lo, lon)
        total = localized[:rows] * pert_ref[0, level].astype(F32)
        for m in range(1, members):
            total += localized[m * rows : (m + 1) * rows] * pert_ref[m, level].astype(F32)
        part[pl.ds(level * groups, groups)] = total.reshape(groups, urows, flon)
        if groups == 1:

            @pl.when(i < lev // 2)
            def _():
                pr_copy((pair + 1 + i) % npairs).start()

            @pl.when(i >= lev // 2)
            def _():
                combine(i - lev // 2, 0)

        else:
            for g in range(groups // 2):
                pr_copy(level * (groups // 2) + g).start()
        return carry

    lax.fori_loop(0, lev, forward, 0)

    for i in range(1, nmem):
        aux_arrival((me + nmem - i) % nmem).wait_recv()
    ah_up = send(
        auxg.at[:, pl.ds(HALO, HALO)],
        auxg.at[:, pl.ds(HALO + urows, HALO)],
        ah_ss.at[0],
        ah_rs.at[0],
        *up,
    )
    ah_down = send(
        auxg.at[:, pl.ds(urows, HALO)], auxg.at[:, pl.ds(0, HALO)], ah_ss.at[1], ah_rs.at[1], *down
    )

    @pl.when(has_up)
    def _():
        ah_up.start()

    @pl.when(has_down)
    def _():
        ah_down.start()

    if groups > 1:
        lax.fori_loop(0, npairs, combine, 0)

    @pl.when(has_down)
    def _():
        ah_up_arrival = send(
            auxg.at[:, pl.ds(HALO, HALO)],
            auxg.at[:, pl.ds(HALO + urows, HALO)],
            ah_ss.at[0],
            ah_rs.at[0],
            *down,
        )
        ah_up_arrival.wait_recv()

    @pl.when(has_up)
    def _():
        ah_down_arrival = send(
            auxg.at[:, pl.ds(urows, HALO)],
            auxg.at[:, pl.ds(0, HALO)],
            ah_ss.at[1],
            ah_rs.at[1],
            *up,
        )
        ah_down_arrival.wait_recv()

    @pl.when(has_up)
    def _():
        ah_up.wait_send()

    @pl.when(has_down)
    def _():
        ah_down.wait_send()

    place = block * urows - HALO + lax.broadcasted_iota(jnp.int32, (erows, LANES), 0)
    inside = (place >= 0) & (place < nlat * rows)
    lane = lax.broadcasted_iota(jnp.int32, (erows, LANES), 1)
    tiles = LANES // cols
    for q in range(flon // LANES):
        first, second = auxg[tiles * q], auxg[tiles * q + 1]
        lhs = jnp.concatenate([first[:, :LANES], second[:, :LANES]], axis=1)
        hi, rest = lhs.astype(BF16), lhs
        rest = rest - hi.astype(F32)
        mid, low = split2(rest)
        out = dot(jnp.concatenate([hi, mid, low], axis=0), spread[...])
        out = out[:erows] + out[erows : 2 * erows] + out[2 * erows :]
        at = slice(q * LANES, (q + 1) * LANES)
        for t in range(STEPS):
            weight = out[:, t * LANES : (t + 1) * LANES]
            value = out[:, (STEPS + t) * LANES : (STEPS + t + 1) * LANES]
            cell = out[:, (2 * STEPS + t) * LANES : (2 * STEPS + t + 1) * LANES]
            hit = cell == (lane % OBLK).astype(F32)
            wts[t, :, at] = jnp.where(hit, weight, 0.0)
            vals[t, :, at] = value
        w0, w1 = first[:, LANES:], second[:, LANES:]
        lower = lane < cols
        c0 = jnp.where(lower, w0, pltpu.roll(w1, cols, 1))
        c1 = jnp.where(lower, pltpu.roll(w0, cols, 1), w1)
        east_in = inside & (lane + q * LANES < flon - 1)
        west_in = inside & (lane + q * LANES > 0)
        coef[0, :, at] = jnp.where(inside, DIFFUSION - 0.5 * c1, 0.0)
        coef[1, :, at] = jnp.where(inside, DIFFUSION + 0.5 * c1, 0.0)
        coef[2, :, at] = jnp.where(east_in, DIFFUSION - 0.5 * c0, 0.0)
        coef[3, :, at] = jnp.where(west_in, DIFFUSION + 0.5 * c0, 0.0)
        coef[4, :, at] = jnp.where(inside, jnp.full((erows, LANES), 1.0 - 4.0 * DIFFUSION, F32), 0.0)

    total = pr[pair]
    for i in range(1, npairs):
        p = (pair + npairs - i) % npairs
        rs_arrival(p).wait_recv()
        total = total + rs[p]
    total = total * scale
    ext[HALO : HALO + urows] = total
    halo_up = send(
        ext.at[pl.ds(HALO, HALO)],
        ext.at[pl.ds(HALO + urows, HALO)],
        halo_ss.at[0],
        halo_rs.at[0],
        *up,
    )
    halo_down = send(
        ext.at[pl.ds(urows, HALO)], ext.at[pl.ds(0, HALO)], halo_ss.at[1], halo_rs.at[1], *down
    )

    @pl.when(has_up)
    def _():
        halo_up.start()

    @pl.when(has_down)
    def _():
        halo_down.start()

    for m in range(nmem):
        itile[m] = total[:, m * cols : (m + 1) * cols]

    def inc_copy(there):
        return send(
            itile.at[there],
            incr.at[my_level, pl.ds(pl.multiple_of(my_row, 8), urows)],
            inc_ss.at[there],
            inc_rs.at[me],
            there,
            z,
        )

    def inc_arrival(source):
        return send(
            itile.at[source],
            incr.at[
                source // groups, pl.ds(pl.multiple_of((source % groups) * urows, 8), urows)
            ],
            inc_ss.at[source],
            inc_rs.at[source],
            source,
            z,
        )

    for i in range(1, nmem):
        inc_copy((me + i) % nmem).start()
    incr[my_level, pl.ds(pl.multiple_of(my_row, 8), urows)] = itile[me]

    @pl.when(has_down)
    def _():
        send(
            ext.at[pl.ds(HALO, HALO)],
            ext.at[pl.ds(HALO + urows, HALO)],
            halo_ss.at[0],
            halo_rs.at[0],
            *down,
        ).wait_recv()

    @pl.when(has_up)
    def _():
        send(
            ext.at[pl.ds(urows, HALO)], ext.at[pl.ds(0, HALO)], halo_ss.at[1], halo_rs.at[1], *up
        ).wait_recv()

    @pl.when(has_up)
    def _():
        halo_up.wait_send()

    @pl.when(has_down)
    def _():
        halo_down.wait_send()

    state = ext[...]
    forcing = []
    for t in range(STEPS):
        state = (
            coef[4] * state
            + coef[0] * pltpu.roll(state, erows - 1, 0)
            + coef[1] * pltpu.roll(state, 1, 0)
            + coef[2] * pltpu.roll(state, flon - 1, 1)
            + coef[3] * pltpu.roll(state, 1, 1)
        )
        wts[t] = wts[t] * (state - vals[t])
    adjoint = None
    for t in reversed(range(STEPS)):
        adjoint = wts[t] if adjoint is None else adjoint + wts[t]
        adjoint = (
            coef[4] * adjoint
            + pltpu.roll(coef[1] * adjoint, erows - 1, 0)
            + pltpu.roll(coef[0] * adjoint, 1, 0)
            + pltpu.roll(coef[3] * adjoint, flon - 1, 1)
            + pltpu.roll(coef[2] * adjoint, 1, 1)
        )
    adjg[me] = adjoint[HALO : HALO + urows]

    def adj_copy(p):
        return send(adjg.at[me], adjg.at[me], adj_ss.at[p], adj_rs.at[pair], 2 * p + core, z)

    def adj_arrival(p):
        unit = 2 * p + core
        return send(adjg.at[unit], adjg.at[unit], adj_ss.at[p], adj_rs.at[p], unit, z)

    def relay(p):
        unit = 2 * p + core
        return send(adjg.at[unit], adjg.at[unit], rel_ss.at[p], rel_rs.at[p], partner, z)

    def relay_arrival(p):
        unit = 2 * p + (1 - core)
        return send(adjg.at[unit], adjg.at[unit], rel_ss.at[p], rel_rs.at[p], partner, z)

    for i in range(1, npairs):
        adj_copy((pair + i) % npairs).start()

    def g_copy(there, level):
        return send(
            gb.at[there, level], gr.at[z, level], g_ss.at[there, level], g_rs.at[z, level], me, there
        )

    def g_arrival(source, level):
        return send(
            gb.at[source, level],
            gr.at[source, level],
            g_ss.at[source, level],
            g_rs.at[source, level],
            me,
            source,
        )

    def backward(level):
        field = adjg[pl.ds(level * groups, groups)].reshape(rows, flon)
        product = jnp.concatenate(
            [pert_ref[m, level].astype(F32) * field for m in range(members)], axis=0
        )
        hi, lo = split2(product)
        over_lon = ((1,), (1,))
        projected = dot(hi, lon, over_lon) + dot(lo, lon, over_lon)
        projected = jnp.concatenate(
            [projected[m * rows : (m + 1) * rows] for m in range(members)], axis=1
        )
        hi, lo = split2(projected)
        banded = dot(lat_t2, jnp.concatenate([hi, lo], axis=0))
        gb[:, level] = banded.reshape(nlat, -1, members * clon)
        for i in range(1, nlat):
            g_copy((z + i) % nlat, level).start()

    def near(i, carry):
        p = (pair + npairs - i) % npairs

        @pl.when(i > 0)
        def _():
            adj_arrival(p).wait_recv()

        relay(p).start()
        if groups == 1:
            backward(2 * p + core)
        return carry

    lax.fori_loop(0, npairs, near, 0)

    def far(i, carry):
        p = (pair + npairs - i) % npairs
        relay_arrival(p).wait_recv()
        if groups == 1:
            backward(2 * p + (1 - core))
        elif groups == 2:
            backward(p)
        else:

            @pl.when(p % (groups // 2) == groups // 2 - 1)
            def _():
                backward(p // (groups // 2))

        return carry

    lax.fori_loop(0, npairs, far, 0)

    for i in range(1, nmem):
        inc_arrival((me + nmem - i) % nmem).wait_recv()
    inc_ref[...] = incr[...]

    def finish(level, carry):
        total = gb[z, level]
        for i in range(1, nlat):
            source = (z + nlat - i) % nlat
            g_arrival(source, level).wait_recv()
            total = total + gr[source, level]
        gb[z, level] = total
        return carry

    lax.fori_loop(0, lev, finish, 0)
    for m in range(members):
        total = jnp.swapaxes(gb[z, :, :, m * clon : (m + 1) * clon], 0, 1)
        grad_ref[:, m] = total * scale + coarse_ref[:, m].astype(F32)

    for i in range(1, nmem):
        aux_copy((me + i) % nmem).wait_send()
        inc_copy((me + i) % nmem).wait_send()
    for p in range(npairs):
        pr_copy(p).wait_send()
        relay(p).wait_send()
    for i in range(1, npairs):
        rs_copy((pair + i) % npairs).wait_send()
        adj_copy((pair + i) % npairs).wait_send()

    def drain(level, carry):
        for i in range(1, nlat):
            cg_copy((z + i) % nlat, level).wait_send()
            g_copy((z + i) % nlat, level).wait_send()
        return carry

    lax.fori_loop(0, lev, drain, 0)


def body(
    nmem,
    nlat,
    coarse_weights,
    perturbations,
    lat_matrix,
    lon_matrix,
    wind_field,
    observed_cell,
    observed_value,
    observed_weight,
):
    members, lev, rows, flon = perturbations.shape
    cband, _, _, clon = coarse_weights.shape
    cols = wind_field.shape[2]
    blocks = cols // OBLK
    groups = nmem // lev
    urows = rows // groups
    erows = urows + 2 * HALO
    npairs = nmem // 2
    assert nmem == lev * groups and nmem % 2 == 0 and urows % 8 == 0 and urows >= HALO
    assert 2 * cols == LANES and 3 * STEPS * blocks <= LANES
    vmem = pl.BlockSpec(memory_space=pltpu.VMEM)
    dma = pltpu.SemaphoreType.DMA
    width = members * clon
    arguments = (
        coarse_weights,
        perturbations,
        lat_matrix,
        lon_matrix,
        wind_field,
        observed_cell,
        observed_value,
        observed_weight,
    )
    return pl.pallas_call(
        functools.partial(kernel, nmem, nlat, float(1.0 / (members * nmem - 1) ** 0.5)),
        out_shape=(
            jax.ShapeDtypeStruct((cband, members, lev, clon), F32),
            jax.ShapeDtypeStruct((lev, rows, cols), F32),
        ),
        in_specs=[pl.BlockSpec(memory_space=pl.ANY)] * len(arguments),
        out_specs=(vmem, vmem),
        scratch_shapes=[
            *[pltpu.VMEM(x.shape, x.dtype) for x in arguments],
            pltpu.VMEM((lev, rows, 2 * LANES), F32),
            pltpu.VMEM((nlat, lev, members, cband, clon), BF16),
            pltpu.VMEM((nmem, erows, 2 * LANES), F32),
            pltpu.VMEM((nmem, urows, flon), F32),
            pltpu.VMEM((npairs, urows, flon), F32),
            pltpu.VMEM((npairs, urows, flon), F32),
            pltpu.VMEM((erows, flon), F32),
            pltpu.VMEM((2 * LANES, 3 * STEPS * LANES), BF16),
            pltpu.VMEM((5, erows, flon), F32),
            pltpu.VMEM((STEPS, erows, flon), F32),
            pltpu.VMEM((STEPS, erows, flon), F32),
            pltpu.VMEM((nmem, urows, cols), F32),
            pltpu.VMEM((lev, rows, cols), F32),
            pltpu.VMEM((nmem, urows, flon), F32),
            pltpu.VMEM((nlat, lev, cband, width), F32),
            pltpu.VMEM((nlat, lev, cband, width), F32),
            dma((len(arguments),)),
            dma((nlat, lev)),
            dma((nlat, lev)),
            dma((nmem,)),
            dma((nmem,)),
            dma((2,)),
            dma((2,)),
            dma((npairs,)),
            dma((npairs,)),
            dma((npairs,)),
            dma((npairs,)),
            dma((2,)),
            dma((2,)),
            dma((nmem,)),
            dma((nmem,)),
            dma((npairs,)),
            dma((npairs,)),
            dma((npairs,)),
            dma((npairs,)),
            dma((nlat, lev)),
            dma((nlat, lev)),
        ],
        compiler_params=pltpu.CompilerParams(
            collective_id=0, has_side_effects=True, vmem_limit_bytes=60 * 1024 * 1024
        ),
    )(*arguments)


def solution(mesh):
    in_specs = (
        P("lat", "mem", None, None),
        P("mem", None, "lat", None),
        P("lat", None),
        P(),
        P(None, "lat", "mem"),
        P(None, None, "lat", "mem"),
        P(None, None, "lat", "mem"),
        P(None, None, "lat", "mem"),
    )
    out_specs = (P("lat", "mem", None, None), P(None, "lat", "mem"))
    call = functools.partial(body, mesh.shape["mem"], mesh.shape["lat"])
    return jax.shard_map(call, mesh=mesh, in_specs=in_specs, out_specs=out_specs, check_vma=False)
```

```python
import functools

import jax
import jax.numpy as jnp
from jax import lax
from jax.experimental import pallas as pl
from jax.experimental.pallas import tpu as pltpu
from jax.sharding import PartitionSpec as P

STEPS = 4
OBLK = 8
HALO = 2 * STEPS
LAG = 3
LANES = 128
DIFFUSION = 0.2
F32 = jnp.float32
BF16 = jnp.bfloat16


def split2(x):
    hi = x.astype(BF16)
    return hi, (x - hi.astype(F32)).astype(BF16)


def dot(a, b, dims=((1,), (0,))):
    return lax.dot_general(a, b, (dims, ((), ())), preferred_element_type=F32)


def kernel(
    nmem,
    nlat,
    scale,
    coarse_hbm,
    pert_hbm,
    lat_hbm,
    lon_hbm,
    wind_hbm,
    cell_hbm,
    value_hbm,
    weight_hbm,
    grad_ref,
    inc_ref,
    coarse_ref,
    pert_ref,
    lat_ref,
    lon_ref,
    wind_ref,
    cell_ref,
    value_ref,
    weight_ref,
    aux_ref,
    cg,
    auxg,
    part,
    pr,
    rs,
    ext,
    spread,
    coef,
    wts,
    vals,
    itile,
    incr,
    adjg,
    gb,
    gr,
    relayed,
    in_sem,
    cg_ss,
    cg_rs,
    aux_ss,
    aux_rs,
    ah_ss,
    ah_rs,
    pr_ss,
    pr_rs,
    rs_ss,
    rs_rs,
    halo_ss,
    halo_rs,
    inc_ss,
    inc_rs,
    adj_ss,
    adj_rs,
    rel_ss,
    rel_rs,
    g_ss,
    g_rs,
    relayed_rs,
):
    members, lev, rows, flon = pert_ref.shape
    clon = lon_ref.shape[0]
    cols = flon // nmem
    groups = nmem // lev
    urows = rows // groups
    erows = urows + 2 * HALO
    npairs = nmem // 2
    me = lax.axis_index("mem")
    z = lax.axis_index("lat")
    pair = me // 2
    core = me % 2
    partner = pair * 2 + (1 - core)
    my_level = me // groups
    my_group = me % groups
    my_row = my_group * urows
    block = z * groups + my_group
    has_up = block > 0
    has_down = block < nlat * groups - 1

    def neighbour(shift):
        there = block + shift
        return (my_level * groups + (there + groups) % groups, (there + groups) // groups - 1)

    up = neighbour(-1)
    down = neighbour(1)

    def send(src, dst, ss, rsem, mem, lat):
        return pltpu.make_async_remote_copy(
            src_ref=src,
            dst_ref=dst,
            send_sem=ss,
            recv_sem=rsem,
            device_id={"mem": mem, "lat": lat},
            device_id_type=pl.DeviceIdType.MESH,
        )

    arguments = (
        (coarse_hbm, coarse_ref),
        (lat_hbm, lat_ref),
        (lon_hbm, lon_ref),
        (wind_hbm, wind_ref),
        (cell_hbm, cell_ref),
        (value_hbm, value_ref),
        (weight_hbm, weight_ref),
        (pert_hbm, pert_ref),
    )
    loads = [
        pltpu.make_async_copy(src, dst, in_sem.at[i]) for i, (src, dst) in enumerate(arguments)
    ]
    for load in loads:
        load.start()

    barrier = pltpu.get_barrier_semaphore()

    def greet(mem, lat):
        pl.semaphore_signal(
            barrier, inc=1, device_id={"mem": mem, "lat": lat}, device_id_type=pl.DeviceIdType.MESH
        )

    for i in range(1, nlat):
        greet(me, (z + i) % nlat)
    for i in range(1, nmem):
        greet((me + i) % nmem, z)
    loads[0].wait()
    for m in range(members):
        mine = jnp.swapaxes(coarse_ref[:, m].astype(F32), 0, 1).astype(BF16)
        for level in range(lev):
            cg[z, level, m] = mine[level]
    pl.semaphore_wait(barrier, nmem + nlat - 2)
    if groups > 1:
        far_up = has_up & (my_group == 0)
        far_down = has_down & (my_group == groups - 1)

        @pl.when(far_up)
        def _():
            greet(*up)

        @pl.when(far_down)
        def _():
            greet(*down)

        @pl.when(far_up)
        def _():
            pl.semaphore_wait(barrier, 1)

        @pl.when(far_down)
        def _():
            pl.semaphore_wait(barrier, 1)

    def level_at(i):
        if groups > 1:
            return i
        half = lev // 2
        p = (pair + 1 + i) % npairs
        return 2 * p + jnp.where(i < half, 1 - core, core)

    def cg_copy(there, level):
        return send(
            cg.at[z, level], cg.at[z, level], cg_ss.at[there, level], cg_rs.at[z, level], me, there
        )

    def cg_arrival(source, level):
        return send(
            cg.at[source, level],
            cg.at[source, level],
            cg_ss.at[source, level],
            cg_rs.at[source, level],
            me,
            source,
        )

    def spread_coarse(i, carry):
        for j in range(1, nlat):
            cg_copy((z + j) % nlat, level_at(i)).start()
        return carry

    lax.fori_loop(0, lev, spread_coarse, 0)

    for load in loads[1:-1]:
        load.wait()

    blank = jnp.zeros((LANES - 3 * STEPS * (cols // OBLK), rows), F32)
    winds = jnp.concatenate([wind_ref[0], wind_ref[1]], axis=1)

    def pack(level, carry):
        pieces = [ref[t, level] for ref in (weight_ref, value_ref) for t in range(STEPS)]
        pieces += [cell_ref[t, level].astype(F32) for t in range(STEPS)]
        aux_ref[level, :, :LANES] = jnp.transpose(jnp.concatenate(pieces + [blank], axis=0))
        aux_ref[level, :, LANES:] = winds
        return carry

    lax.fori_loop(0, lev, pack, 0)

    def aux_copy(there):
        return send(
            aux_ref.at[there // groups, pl.ds(pl.multiple_of((there % groups) * urows, 8), urows)],
            auxg.at[me, pl.ds(HALO, urows)],
            aux_ss.at[there],
            aux_rs.at[me],
            there,
            z,
        )

    def aux_arrival(source):
        return send(
            aux_ref.at[0, pl.ds(0, urows)],
            auxg.at[source, pl.ds(HALO, urows)],
            aux_ss.at[source],
            aux_rs.at[source],
            source,
            z,
        )

    for i in range(1, nmem):
        aux_copy((me + i) % nmem).start()

    auxg[me, HALO : HALO + urows] = aux_ref[my_level, pl.ds(pl.multiple_of(my_row, 8), urows)]

    @pl.when(jnp.logical_not(has_up))
    def _():
        auxg[:, :HALO] = jnp.zeros((nmem, HALO, 2 * LANES), F32)
        ext[:HALO] = jnp.zeros((HALO, flon), F32)

    @pl.when(jnp.logical_not(has_down))
    def _():
        auxg[:, HALO + urows :] = jnp.zeros((nmem, HALO, 2 * LANES), F32)
        ext[HALO + urows :] = jnp.zeros((HALO, flon), F32)

    per_tile = cols // OBLK
    k = lax.broadcasted_iota(jnp.int32, (2 * LANES, LANES), 0)
    n = lax.broadcasted_iota(jnp.int32, (2 * LANES, LANES), 1)
    for piece in range(3 * STEPS):
        hit = k == (n // cols) * LANES + piece * per_tile + (n % cols) // OBLK
        spread[:, piece * LANES : (piece + 1) * LANES] = jnp.where(hit, 1.0, 0.0).astype(BF16)

    lat_f32 = lat_ref[...].astype(F32)
    lat_bf = lat_ref[...]
    lat_t = jnp.transpose(lat_f32).astype(BF16)
    lat_t2 = jnp.concatenate([lat_t, lat_t], axis=1)
    lon = lon_ref[...]

    loads[-1].wait()

    def pr_copy(p):
        unit = 2 * p + (1 - core)
        return send(part.at[unit], pr.at[p], pr_ss.at[p], pr_rs.at[p], partner, z)

    def pr_arrival(p):
        return send(part.at[2 * p + core], pr.at[p], pr_ss.at[p], pr_rs.at[p], partner, z)

    def rs_copy(p):
        return send(pr.at[p], rs.at[pair], rs_ss.at[p], rs_rs.at[pair], 2 * p + core, z)

    def rs_arrival(p):
        return send(pr.at[p], rs.at[p], rs_ss.at[p], rs_rs.at[p], 2 * p + core, z)

    def combine(i, carry):
        p = (pair + 1 + i) % npairs
        pr_arrival(p).wait_recv()
        pr[p] = pr[p] + part[2 * p + core]

        @pl.when(p != pair)
        def _():
            rs_copy(p).start()

        return carry

    def forward(i, carry):
        level = level_at(i)
        for j in range(1, nlat):
            cg_arrival((z + nlat - j) % nlat, level).wait_recv()
        coarse = jnp.concatenate(
            [cg[:, level, m].astype(F32).reshape(-1, clon) for m in range(members)], axis=1
        ).astype(BF16)
        partly = dot(lat_bf, coarse)
        partly = jnp.concatenate(
            [partly[:, m * clon : (m + 1) * clon] for m in range(members)], axis=0
        )
        hi, lo = split2(partly)
        localized = dot(hi, lon) + dot(lo, lon)
        total = localized[:rows] * pert_ref[0, level].astype(F32)
        for m in range(1, members):
            total += localized[m * rows : (m + 1) * rows] * pert_ref[m, level].astype(F32)
        part[pl.ds(level * groups, groups)] = total.reshape(groups, urows, flon)
        if groups == 1:

            @pl.when(i < lev // 2)
            def _():
                pr_copy((pair + 1 + i) % npairs).start()

            @pl.when(i >= lev // 2)
            def _():
                combine(i - lev // 2, 0)

        else:
            for g in range(groups // 2):
                pr_copy(level * (groups // 2) + g).start()
        return carry

    lax.fori_loop(0, lev, forward, 0)

    for i in range(1, nmem):
        aux_arrival((me + nmem - i) % nmem).wait_recv()
    ah_up = send(
        auxg.at[:, pl.ds(HALO, HALO)],
        auxg.at[:, pl.ds(HALO + urows, HALO)],
        ah_ss.at[0],
        ah_rs.at[0],
        *up,
    )
    ah_down = send(
        auxg.at[:, pl.ds(urows, HALO)], auxg.at[:, pl.ds(0, HALO)], ah_ss.at[1], ah_rs.at[1], *down
    )

    @pl.when(has_up)
    def _():
        ah_up.start()

    @pl.when(has_down)
    def _():
        ah_down.start()

    if groups > 1:
        lax.fori_loop(0, npairs, combine, 0)

    @pl.when(has_down)
    def _():
        ah_up_arrival = send(
            auxg.at[:, pl.ds(HALO, HALO)],
            auxg.at[:, pl.ds(HALO + urows, HALO)],
            ah_ss.at[0],
            ah_rs.at[0],
            *down,
        )
        ah_up_arrival.wait_recv()

    @pl.when(has_up)
    def _():
        ah_down_arrival = send(
            auxg.at[:, pl.ds(urows, HALO)],
            auxg.at[:, pl.ds(0, HALO)],
            ah_ss.at[1],
            ah_rs.at[1],
            *up,
        )
        ah_down_arrival.wait_recv()

    @pl.when(has_up)
    def _():
        ah_up.wait_send()

    @pl.when(has_down)
    def _():
        ah_down.wait_send()

    place = block * urows - HALO + lax.broadcasted_iota(jnp.int32, (erows, LANES), 0)
    inside = (place >= 0) & (place < nlat * rows)
    lane = lax.broadcasted_iota(jnp.int32, (erows, LANES), 1)
    tiles = LANES // cols
    for q in range(flon // LANES):
        first, second = auxg[tiles * q], auxg[tiles * q + 1]
        lhs = jnp.concatenate([first[:, :LANES], second[:, :LANES]], axis=1)
        hi, rest = lhs.astype(BF16), lhs
        rest = rest - hi.astype(F32)
        mid, low = split2(rest)
        out = dot(jnp.concatenate([hi, mid, low], axis=0), spread[...])
        out = out[:erows] + out[erows : 2 * erows] + out[2 * erows :]
        at = slice(q * LANES, (q + 1) * LANES)
        for t in range(STEPS):
            weight = out[:, t * LANES : (t + 1) * LANES]
            value = out[:, (STEPS + t) * LANES : (STEPS + t + 1) * LANES]
            cell = out[:, (2 * STEPS + t) * LANES : (2 * STEPS + t + 1) * LANES]
            hit = cell == (lane % OBLK).astype(F32)
            wts[t, :, at] = jnp.where(hit, weight, 0.0)
            vals[t, :, at] = value
        w0, w1 = first[:, LANES:], second[:, LANES:]
        lower = lane < cols
        c0 = jnp.where(lower, w0, pltpu.roll(w1, cols, 1))
        c1 = jnp.where(lower, pltpu.roll(w0, cols, 1), w1)
        east_in = inside & (lane + q * LANES < flon - 1)
        west_in = inside & (lane + q * LANES > 0)
        coef[0, :, at] = jnp.where(inside, DIFFUSION - 0.5 * c1, 0.0)
        coef[1, :, at] = jnp.where(inside, DIFFUSION + 0.5 * c1, 0.0)
        coef[2, :, at] = jnp.where(east_in, DIFFUSION - 0.5 * c0, 0.0)
        coef[3, :, at] = jnp.where(west_in, DIFFUSION + 0.5 * c0, 0.0)
        coef[4, :, at] = jnp.where(inside, jnp.full((erows, LANES), 1.0 - 4.0 * DIFFUSION, F32), 0.0)

    total = pr[pair]
    for i in range(1, npairs):
        p = (pair + npairs - i) % npairs
        rs_arrival(p).wait_recv()
        total = total + rs[p]
    total = total * scale
    ext[HALO : HALO + urows] = total
    halo_up = send(
        ext.at[pl.ds(HALO, HALO)],
        ext.at[pl.ds(HALO + urows, HALO)],
        halo_ss.at[0],
        halo_rs.at[0],
        *up,
    )
    halo_down = send(
        ext.at[pl.ds(urows, HALO)], ext.at[pl.ds(0, HALO)], halo_ss.at[1], halo_rs.at[1], *down
    )

    @pl.when(has_up)
    def _():
        halo_up.start()

    @pl.when(has_down)
    def _():
        halo_down.start()

    for m in range(nmem):
        itile[m] = total[:, m * cols : (m + 1) * cols]

    def inc_copy(there):
        return send(
            itile.at[there],
            incr.at[my_level, pl.ds(pl.multiple_of(my_row, 8), urows)],
            inc_ss.at[there],
            inc_rs.at[me],
            there,
            z,
        )

    def inc_arrival(source):
        return send(
            itile.at[source],
            incr.at[
                source // groups, pl.ds(pl.multiple_of((source % groups) * urows, 8), urows)
            ],
            inc_ss.at[source],
            inc_rs.at[source],
            source,
            z,
        )

    for i in range(1, nmem):
        inc_copy((me + i) % nmem).start()
    incr[my_level, pl.ds(pl.multiple_of(my_row, 8), urows)] = itile[me]

    @pl.when(has_down)
    def _():
        send(
            ext.at[pl.ds(HALO, HALO)],
            ext.at[pl.ds(HALO + urows, HALO)],
            halo_ss.at[0],
            halo_rs.at[0],
            *down,
        ).wait_recv()

    @pl.when(has_up)
    def _():
        send(
            ext.at[pl.ds(urows, HALO)], ext.at[pl.ds(0, HALO)], halo_ss.at[1], halo_rs.at[1], *up
        ).wait_recv()

    @pl.when(has_up)
    def _():
        halo_up.wait_send()

    @pl.when(has_down)
    def _():
        halo_down.wait_send()

    state = ext[...]
    forcing = []
    for t in range(STEPS):
        state = (
            coef[4] * state
            + coef[0] * pltpu.roll(state, erows - 1, 0)
            + coef[1] * pltpu.roll(state, 1, 0)
            + coef[2] * pltpu.roll(state, flon - 1, 1)
            + coef[3] * pltpu.roll(state, 1, 1)
        )
        wts[t] = wts[t] * (state - vals[t])
    adjoint = None
    for t in reversed(range(STEPS)):
        adjoint = wts[t] if adjoint is None else adjoint + wts[t]
        adjoint = (
            coef[4] * adjoint
            + pltpu.roll(coef[1] * adjoint, erows - 1, 0)
            + pltpu.roll(coef[0] * adjoint, 1, 0)
            + pltpu.roll(coef[3] * adjoint, flon - 1, 1)
            + pltpu.roll(coef[2] * adjoint, 1, 1)
        )
    adjg[me] = adjoint[HALO : HALO + urows]

    def adj_copy(p):
        return send(adjg.at[me], adjg.at[me], adj_ss.at[p], adj_rs.at[pair], 2 * p + core, z)

    def adj_arrival(p):
        unit = 2 * p + core
        return send(adjg.at[unit], adjg.at[unit], adj_ss.at[p], adj_rs.at[p], unit, z)

    def relay(p):
        unit = 2 * p + core
        return send(adjg.at[unit], adjg.at[unit], rel_ss.at[p], rel_rs.at[p], partner, z)

    def relay_arrival(p):
        unit = 2 * p + (1 - core)
        return send(adjg.at[unit], adjg.at[unit], rel_ss.at[p], rel_rs.at[p], partner, z)

    for i in range(1, npairs):
        adj_copy((pair + i) % npairs).start()

    directions = ((0, 1), (1, -1))

    def g_target(way, step, k, there, level):
        if k >= 3:
            return z + step, relayed.at[way, there, level], relayed_rs.at[way, there, level]
        slot = 2 * way + k - 1
        return there, gr.at[slot, level], g_rs.at[slot, level]

    def g_copy(way, step, k, level):
        there = z + step * k
        lat, dst, arrived = g_target(way, step, k, there, level)
        return send(gb.at[there, level], dst, g_ss.at[there, level], arrived, me, lat)

    def exists(place):
        return (place >= 0) & (place < nlat)

    def g_first(level):
        for k in range(nlat - 1, 0, -1):
            for way, step in directions:
                ready = exists(z + step * k)
                if k > 1:
                    ready = ready & jnp.logical_not(exists(z - step))

                @pl.when(ready)
                def _():
                    g_copy(way, step, k, level).start()

    def g_later(level):
        for k in range(nlat - 2, 1, -1):
            for way, step in directions:
                there = z + step * k

                @pl.when(exists(there) & exists(z - step))
                def _():
                    send(
                        gb.at[there, level],
                        relayed.at[way, there, level],
                        g_ss.at[there, level],
                        relayed_rs.at[way, there, level],
                        me,
                        z - step,
                    ).wait_recv()
                    gb[there, level] = gb[there, level] + relayed[way, there, level]
                    g_copy(way, step, k, level).start()

    def backward(level):
        field = adjg[pl.ds(level * groups, groups)].reshape(rows, flon)
        product = jnp.concatenate(
            [pert_ref[m, level].astype(F32) * field for m in range(members)], axis=0
        )
        hi, lo = split2(product)
        over_lon = ((1,), (1,))
        projected = dot(hi, lon, over_lon) + dot(lo, lon, over_lon)
        projected = jnp.concatenate(
            [projected[m * rows : (m + 1) * rows] for m in range(members)], axis=1
        )
        hi, lo = split2(projected)
        banded = dot(lat_t2, jnp.concatenate([hi, lo], axis=0))
        gb[:, level] = banded.reshape(nlat, -1, members * clon)
        g_first(level)

    def order(j):
        p = (pair + 2 * npairs - j) % npairs
        if groups == 2:
            return p
        return 2 * p + jnp.where(j < npairs, core, 1 - core)

    def step_back(j):
        backward(order(j))

        @pl.when(j >= LAG)
        def _():
            g_later(order(j - LAG))

    def near(i, carry):
        p = (pair + npairs - i) % npairs

        @pl.when(i > 0)
        def _():
            adj_arrival(p).wait_recv()

        relay(p).start()
        if groups == 1:
            step_back(i)
        return carry

    lax.fori_loop(0, npairs, near, 0)

    def far(i, carry):
        p = (pair + npairs - i) % npairs
        relay_arrival(p).wait_recv()
        step_back(npairs + i if groups == 1 else i)
        return carry

    lax.fori_loop(0, npairs, far, 0)

    def trail(j, carry):
        g_later(order(j))
        return carry

    lax.fori_loop(lev - LAG, lev, trail, 0)

    for i in range(1, nmem):
        inc_arrival((me + nmem - i) % nmem).wait_recv()
    inc_ref[...] = incr[...]

    def finish(j, carry):
        level = order(j)
        for k in range(1, min(3, nlat)):
            for way, step in directions:
                source = z - step * k
                slot = 2 * way + k - 1

                @pl.when(exists(source))
                def _():
                    send(
                        gb.at[z, level],
                        gr.at[slot, level],
                        g_ss.at[z, level],
                        g_rs.at[slot, level],
                        me,
                        source,
                    ).wait_recv()
                    gb[z, level] = gb[z, level] + gr[slot, level]

        return carry

    lax.fori_loop(0, lev, finish, 0)
    for m in range(members):
        total = jnp.swapaxes(gb[z, :, :, m * clon : (m + 1) * clon], 0, 1)
        grad_ref[:, m] = total * scale

    for i in range(1, nmem):
        aux_copy((me + i) % nmem).wait_send()
        inc_copy((me + i) % nmem).wait_send()
    for p in range(npairs):
        pr_copy(p).wait_send()
        relay(p).wait_send()
    for i in range(1, npairs):
        rs_copy((pair + i) % npairs).wait_send()
        adj_copy((pair + i) % npairs).wait_send()

    def drain(level, carry):
        for i in range(1, nlat):
            there = (z + i) % nlat
            cg_copy(there, level).wait_send()
            send(
                gb.at[there, level],
                gr.at[0, level],
                g_ss.at[there, level],
                g_rs.at[0, level],
                me,
                there,
            ).wait_send()
        return carry

    lax.fori_loop(0, lev, drain, 0)


def body(
    nmem,
    nlat,
    coarse_weights,
    perturbations,
    lat_matrix,
    lon_matrix,
    wind_field,
    observed_cell,
    observed_value,
    observed_weight,
):
    members, lev, rows, flon = perturbations.shape
    cband, _, _, clon = coarse_weights.shape
    cols = wind_field.shape[2]
    blocks = cols // OBLK
    groups = nmem // lev
    urows = rows // groups
    erows = urows + 2 * HALO
    npairs = nmem // 2
    assert nmem == lev * groups and nmem % 2 == 0 and groups <= 2 and urows % 8 == 0 and urows >= HALO
    assert 2 * cols == LANES and 3 * STEPS * blocks <= LANES
    vmem = pl.BlockSpec(memory_space=pltpu.VMEM)
    dma = pltpu.SemaphoreType.DMA
    width = members * clon
    arguments = (
        coarse_weights,
        perturbations,
        lat_matrix,
        lon_matrix,
        wind_field,
        jnp.swapaxes(observed_cell, 2, 3),
        jnp.swapaxes(observed_value, 2, 3),
        jnp.swapaxes(observed_weight, 2, 3),
    )
    banded, increment = pl.pallas_call(
        functools.partial(kernel, nmem, nlat, float(1.0 / (members * nmem - 1) ** 0.5)),
        out_shape=(
            jax.ShapeDtypeStruct((cband, members, lev, clon), F32),
            jax.ShapeDtypeStruct((lev, rows, cols), F32),
        ),
        in_specs=[pl.BlockSpec(memory_space=pltpu.HBM)] * len(arguments),
        out_specs=(vmem, vmem),
        scratch_shapes=[
            *[pltpu.VMEM(x.shape, x.dtype) for x in arguments],
            pltpu.VMEM((lev, rows, 2 * LANES), F32),
            pltpu.VMEM((nlat, lev, members, cband, clon), BF16),
            pltpu.VMEM((nmem, erows, 2 * LANES), F32),
            pltpu.VMEM((nmem, urows, flon), F32),
            pltpu.VMEM((npairs, urows, flon), F32),
            pltpu.VMEM((npairs, urows, flon), F32),
            pltpu.VMEM((erows, flon), F32),
            pltpu.VMEM((2 * LANES, 3 * STEPS * LANES), BF16),
            pltpu.VMEM((5, erows, flon), F32),
            pltpu.VMEM((STEPS, erows, flon), F32),
            pltpu.VMEM((STEPS, erows, flon), F32),
            pltpu.VMEM((nmem, urows, cols), F32),
            pltpu.VMEM((lev, rows, cols), F32),
            pltpu.VMEM((nmem, urows, flon), F32),
            pltpu.VMEM((nlat, lev, cband, width), F32),
            pltpu.VMEM((4, lev, cband, width), F32),
            pltpu.VMEM((2, nlat, lev, cband, width), F32),
            dma((len(arguments),)),
            dma((nlat, lev)),
            dma((nlat, lev)),
            dma((nmem,)),
            dma((nmem,)),
            dma((2,)),
            dma((2,)),
            dma((npairs,)),
            dma((npairs,)),
            dma((npairs,)),
            dma((npairs,)),
            dma((2,)),
            dma((2,)),
            dma((nmem,)),
            dma((nmem,)),
            dma((npairs,)),
            dma((npairs,)),
            dma((npairs,)),
            dma((npairs,)),
            dma((nlat, lev)),
            dma((4, lev)),
            dma((2, nlat, lev)),
        ],
        compiler_params=pltpu.CompilerParams(
            collective_id=0, has_side_effects=True, vmem_limit_bytes=60 * 1024 * 1024
        ),
    )(*arguments)
    return banded + coarse_weights.astype(F32), increment


def solution(mesh):
    in_specs = (
        P("lat", "mem", None, None),
        P("mem", None, "lat", None),
        P("lat", None),
        P(),
        P(None, "lat", "mem"),
        P(None, None, "lat", "mem"),
        P(None, None, "lat", "mem"),
        P(None, None, "lat", "mem"),
    )
    out_specs = (P("lat", "mem", None, None), P(None, "lat", "mem"))
    call = functools.partial(body, mesh.shape["mem"], mesh.shape["lat"])
    return jax.shard_map(call, mesh=mesh, in_specs=in_specs, out_specs=out_specs, check_vma=False)
```

```python
import functools

import jax
import jax.numpy as jnp
from jax import lax
from jax.experimental import pallas as pl
from jax.experimental.pallas import tpu as pltpu
from jax.sharding import PartitionSpec as P

STEPS = 4
OBLK = 8
HALO = 2 * STEPS
LAG = 3
LANES = 128
DIFFUSION = 0.2
F32 = jnp.float32
BF16 = jnp.bfloat16


def split2(x):
    hi = x.astype(BF16)
    return hi, (x - hi.astype(F32)).astype(BF16)


def dot(a, b, dims=((1,), (0,))):
    return lax.dot_general(a, b, (dims, ((), ())), preferred_element_type=F32)


def kernel(
    nmem,
    nlat,
    scale,
    coarse_hbm,
    pert_hbm,
    lat_hbm,
    lon_hbm,
    wind_hbm,
    cell_hbm,
    value_hbm,
    weight_hbm,
    grad_ref,
    inc_ref,
    coarse_ref,
    pert_ref,
    lat_ref,
    lon_ref,
    wind_ref,
    cell_ref,
    value_ref,
    weight_ref,
    aux_ref,
    cg,
    auxg,
    part,
    pr,
    rs,
    ext,
    spread,
    coef,
    wts,
    vals,
    itile,
    incr,
    adjg,
    gb,
    gr,
    relayed,
    lon_t,
    in_sem,
    cg_ss,
    cg_rs,
    aux_ss,
    aux_rs,
    ah_ss,
    ah_rs,
    pr_ss,
    pr_rs,
    rs_ss,
    rs_rs,
    halo_ss,
    halo_rs,
    inc_ss,
    inc_rs,
    adj_ss,
    adj_rs,
    rel_ss,
    rel_rs,
    g_ss,
    g_rs,
    relayed_rs,
):
    members, lev, rows, flon = pert_ref.shape
    clon = lon_ref.shape[0]
    cols = flon // nmem
    groups = nmem // lev
    urows = rows // groups
    erows = urows + 2 * HALO
    npairs = nmem // 2
    me = lax.axis_index("mem")
    z = lax.axis_index("lat")
    pair = me // 2
    core = me % 2
    partner = pair * 2 + (1 - core)
    my_level = me // groups
    my_group = me % groups
    my_row = my_group * urows
    block = z * groups + my_group
    has_up = block > 0
    has_down = block < nlat * groups - 1

    def neighbour(shift):
        there = block + shift
        return (my_level * groups + (there + groups) % groups, (there + groups) // groups - 1)

    up = neighbour(-1)
    down = neighbour(1)

    def send(src, dst, ss, rsem, mem, lat):
        return pltpu.make_async_remote_copy(
            src_ref=src,
            dst_ref=dst,
            send_sem=ss,
            recv_sem=rsem,
            device_id={"mem": mem, "lat": lat},
            device_id_type=pl.DeviceIdType.MESH,
        )

    arguments = (
        (coarse_hbm, coarse_ref),
        (lat_hbm, lat_ref),
        (lon_hbm, lon_ref),
        (wind_hbm, wind_ref),
        (cell_hbm, cell_ref),
        (value_hbm, value_ref),
        (weight_hbm, weight_ref),
        (pert_hbm, pert_ref),
    )
    loads = [
        pltpu.make_async_copy(src, dst, in_sem.at[i]) for i, (src, dst) in enumerate(arguments)
    ]
    for load in loads:
        load.start()

    barrier = pltpu.get_barrier_semaphore()

    def greet(mem, lat):
        pl.semaphore_signal(
            barrier, inc=1, device_id={"mem": mem, "lat": lat}, device_id_type=pl.DeviceIdType.MESH
        )

    for i in range(1, nlat):
        greet(me, (z + i) % nlat)
    for i in range(1, nmem):
        greet((me + i) % nmem, z)
    loads[0].wait()
    for m in range(members):
        mine = jnp.swapaxes(coarse_ref[:, m].astype(F32), 0, 1).astype(BF16)
        for level in range(lev):
            cg[z, level, m] = mine[level]
    pl.semaphore_wait(barrier, nmem + nlat - 2)
    if groups > 1:
        far_up = has_up & (my_group == 0)
        far_down = has_down & (my_group == groups - 1)

        @pl.when(far_up)
        def _():
            greet(*up)

        @pl.when(far_down)
        def _():
            greet(*down)

        @pl.when(far_up)
        def _():
            pl.semaphore_wait(barrier, 1)

        @pl.when(far_down)
        def _():
            pl.semaphore_wait(barrier, 1)

    def level_at(i):
        if groups > 1:
            return i
        half = lev // 2
        p = (pair + 1 + i) % npairs
        return 2 * p + jnp.where(i < half, 1 - core, core)

    def cg_copy(there, level):
        return send(
            cg.at[z, level], cg.at[z, level], cg_ss.at[there, level], cg_rs.at[z, level], me, there
        )

    def cg_arrival(source, level):
        return send(
            cg.at[source, level],
            cg.at[source, level],
            cg_ss.at[source, level],
            cg_rs.at[source, level],
            me,
            source,
        )

    def spread_coarse(i, carry):
        for j in range(1, nlat):
            cg_copy((z + j) % nlat, level_at(i)).start()
        return carry

    lax.fori_loop(0, lev, spread_coarse, 0)

    for load in loads[1:-1]:
        load.wait()

    blank = jnp.zeros((LANES - 3 * STEPS * (cols // OBLK), rows), F32)
    winds = jnp.concatenate([wind_ref[0], wind_ref[1]], axis=1)

    def pack(level, carry):
        pieces = [ref[t, level] for ref in (weight_ref, value_ref) for t in range(STEPS)]
        pieces += [cell_ref[t, level].astype(F32) for t in range(STEPS)]
        aux_ref[level, :, :LANES] = jnp.transpose(jnp.concatenate(pieces + [blank], axis=0))
        aux_ref[level, :, LANES:] = winds
        return carry

    lax.fori_loop(0, lev, pack, 0)

    def aux_copy(there):
        return send(
            aux_ref.at[there // groups, pl.ds(pl.multiple_of((there % groups) * urows, 8), urows)],
            auxg.at[me, pl.ds(HALO, urows)],
            aux_ss.at[there],
            aux_rs.at[me],
            there,
            z,
        )

    def aux_arrival(source):
        return send(
            aux_ref.at[0, pl.ds(0, urows)],
            auxg.at[source, pl.ds(HALO, urows)],
            aux_ss.at[source],
            aux_rs.at[source],
            source,
            z,
        )

    for i in range(1, nmem):
        aux_copy((me + i) % nmem).start()

    auxg[me, HALO : HALO + urows] = aux_ref[my_level, pl.ds(pl.multiple_of(my_row, 8), urows)]

    @pl.when(jnp.logical_not(has_up))
    def _():
        auxg[:, :HALO] = jnp.zeros((nmem, HALO, 2 * LANES), F32)
        ext[:HALO] = jnp.zeros((HALO, flon), F32)

    @pl.when(jnp.logical_not(has_down))
    def _():
        auxg[:, HALO + urows :] = jnp.zeros((nmem, HALO, 2 * LANES), F32)
        ext[HALO + urows :] = jnp.zeros((HALO, flon), F32)

    per_tile = cols // OBLK
    k = lax.broadcasted_iota(jnp.int32, (2 * LANES, LANES), 0)
    n = lax.broadcasted_iota(jnp.int32, (2 * LANES, LANES), 1)
    for piece in range(3 * STEPS):
        hit = k == (n // cols) * LANES + piece * per_tile + (n % cols) // OBLK
        spread[:, piece * LANES : (piece + 1) * LANES] = jnp.where(hit, 1.0, 0.0).astype(BF16)

    lat_f32 = lat_ref[...].astype(F32)
    lat_bf = lat_ref[...]
    lat_t = jnp.transpose(lat_f32).astype(BF16)
    lat_t2 = jnp.concatenate([lat_t, lat_t], axis=1)
    lon = lon_ref[...]
    lon_t[...] = jnp.transpose(lon.astype(F32)).astype(BF16)

    loads[-1].wait()

    def pr_copy(p):
        unit = 2 * p + (1 - core)
        return send(part.at[unit], pr.at[p], pr_ss.at[p], pr_rs.at[p], partner, z)

    def pr_arrival(p):
        return send(part.at[2 * p + core], pr.at[p], pr_ss.at[p], pr_rs.at[p], partner, z)

    def rs_copy(p):
        return send(pr.at[p], rs.at[pair], rs_ss.at[p], rs_rs.at[pair], 2 * p + core, z)

    def rs_arrival(p):
        return send(pr.at[p], rs.at[p], rs_ss.at[p], rs_rs.at[p], 2 * p + core, z)

    def combine(i, carry):
        p = (pair + 1 + i) % npairs
        pr_arrival(p).wait_recv()
        pr[p] = pr[p] + part[2 * p + core]

        @pl.when(p != pair)
        def _():
            rs_copy(p).start()

        return carry

    ah_up = send(
        auxg.at[:, pl.ds(HALO, HALO)],
        auxg.at[:, pl.ds(HALO + urows, HALO)],
        ah_ss.at[0],
        ah_rs.at[0],
        *up,
    )
    ah_down = send(
        auxg.at[:, pl.ds(urows, HALO)], auxg.at[:, pl.ds(0, HALO)], ah_ss.at[1], ah_rs.at[1], *down
    )


    def exchange_aux():
        for i in range(1, nmem):
            aux_arrival((me + nmem - i) % nmem).wait_recv()

        @pl.when(has_up)
        def _():
            ah_up.start()

        @pl.when(has_down)
        def _():
            ah_down.start()

    def forward(i, carry):
        level = level_at(i)
        for j in range(1, nlat):
            cg_arrival((z + nlat - j) % nlat, level).wait_recv()
        coarse = jnp.concatenate(
            [cg[:, level, m].astype(F32).reshape(-1, clon) for m in range(members)], axis=1
        ).astype(BF16)
        partly = dot(lat_bf, coarse)
        partly = jnp.concatenate(
            [partly[:, m * clon : (m + 1) * clon] for m in range(members)], axis=0
        )
        hi, lo = split2(partly)
        localized = dot(jnp.concatenate([hi, lo], axis=0), lon)
        localized = localized[: members * rows] + localized[members * rows :]
        total = localized[:rows] * pert_ref[0, level].astype(F32)
        for m in range(1, members):
            total += localized[m * rows : (m + 1) * rows] * pert_ref[m, level].astype(F32)
        part[pl.ds(level * groups, groups)] = total.reshape(groups, urows, flon)

        @pl.when(i == lev // 2)
        def _():
            exchange_aux()

        if groups == 1:

            @pl.when(i < lev // 2)
            def _():
                pr_copy((pair + 1 + i) % npairs).start()

            @pl.when(i >= lev // 2)
            def _():
                combine(i - lev // 2, 0)

        else:
            for g in range(groups // 2):
                pr_copy(level * (groups // 2) + g).start()
        return carry

    lax.fori_loop(0, lev, forward, 0)

    if groups > 1:
        lax.fori_loop(0, npairs, combine, 0)

    @pl.when(has_down)
    def _():
        ah_up_arrival = send(
            auxg.at[:, pl.ds(HALO, HALO)],
            auxg.at[:, pl.ds(HALO + urows, HALO)],
            ah_ss.at[0],
            ah_rs.at[0],
            *down,
        )
        ah_up_arrival.wait_recv()

    @pl.when(has_up)
    def _():
        ah_down_arrival = send(
            auxg.at[:, pl.ds(urows, HALO)],
            auxg.at[:, pl.ds(0, HALO)],
            ah_ss.at[1],
            ah_rs.at[1],
            *up,
        )
        ah_down_arrival.wait_recv()

    @pl.when(has_up)
    def _():
        ah_up.wait_send()

    @pl.when(has_down)
    def _():
        ah_down.wait_send()

    place = block * urows - HALO + lax.broadcasted_iota(jnp.int32, (erows, LANES), 0)
    inside = (place >= 0) & (place < nlat * rows)
    lane = lax.broadcasted_iota(jnp.int32, (erows, LANES), 1)
    tiles = LANES // cols
    for q in range(flon // LANES):
        first, second = auxg[tiles * q], auxg[tiles * q + 1]
        lhs = jnp.concatenate([first[:, :LANES], second[:, :LANES]], axis=1)
        hi, rest = lhs.astype(BF16), lhs
        rest = rest - hi.astype(F32)
        mid, low = split2(rest)
        out = dot(jnp.concatenate([hi, mid, low], axis=0), spread[...])
        out = out[:erows] + out[erows : 2 * erows] + out[2 * erows :]
        at = slice(q * LANES, (q + 1) * LANES)
        for t in range(STEPS):
            weight = out[:, t * LANES : (t + 1) * LANES]
            value = out[:, (STEPS + t) * LANES : (STEPS + t + 1) * LANES]
            cell = out[:, (2 * STEPS + t) * LANES : (2 * STEPS + t + 1) * LANES]
            hit = cell == (lane % OBLK).astype(F32)
            wts[t, :, at] = jnp.where(hit, weight, 0.0)
            vals[t, :, at] = value
        w0, w1 = first[:, LANES:], second[:, LANES:]
        lower = lane < cols
        c0 = jnp.where(lower, w0, pltpu.roll(w1, cols, 1))
        c1 = jnp.where(lower, pltpu.roll(w0, cols, 1), w1)
        east_in = inside & (lane + q * LANES < flon - 1)
        west_in = inside & (lane + q * LANES > 0)
        coef[0, :, at] = jnp.where(inside, DIFFUSION - 0.5 * c1, 0.0)
        coef[1, :, at] = jnp.where(inside, DIFFUSION + 0.5 * c1, 0.0)
        coef[2, :, at] = jnp.where(east_in, DIFFUSION - 0.5 * c0, 0.0)
        coef[3, :, at] = jnp.where(west_in, DIFFUSION + 0.5 * c0, 0.0)
        coef[4, :, at] = jnp.where(inside, jnp.full((erows, LANES), 1.0 - 4.0 * DIFFUSION, F32), 0.0)

    total = pr[pair]
    for i in range(1, npairs):
        p = (pair + npairs - i) % npairs
        rs_arrival(p).wait_recv()
        total = total + rs[p]
    total = total * scale
    ext[HALO : HALO + urows] = total
    halo_up = send(
        ext.at[pl.ds(HALO, HALO)],
        ext.at[pl.ds(HALO + urows, HALO)],
        halo_ss.at[0],
        halo_rs.at[0],
        *up,
    )
    halo_down = send(
        ext.at[pl.ds(urows, HALO)], ext.at[pl.ds(0, HALO)], halo_ss.at[1], halo_rs.at[1], *down
    )

    @pl.when(has_up)
    def _():
        halo_up.start()

    @pl.when(has_down)
    def _():
        halo_down.start()

    for m in range(nmem):
        itile[m] = total[:, m * cols : (m + 1) * cols]

    def inc_copy(there):
        return send(
            itile.at[there],
            incr.at[my_level, pl.ds(pl.multiple_of(my_row, 8), urows)],
            inc_ss.at[there],
            inc_rs.at[me],
            there,
            z,
        )

    def inc_arrival(source):
        return send(
            itile.at[source],
            incr.at[
                source // groups, pl.ds(pl.multiple_of((source % groups) * urows, 8), urows)
            ],
            inc_ss.at[source],
            inc_rs.at[source],
            source,
            z,
        )

    for i in range(1, nmem):
        inc_copy((me + i) % nmem).start()
    incr[my_level, pl.ds(pl.multiple_of(my_row, 8), urows)] = itile[me]

    @pl.when(has_down)
    def _():
        send(
            ext.at[pl.ds(HALO, HALO)],
            ext.at[pl.ds(HALO + urows, HALO)],
            halo_ss.at[0],
            halo_rs.at[0],
            *down,
        ).wait_recv()

    @pl.when(has_up)
    def _():
        send(
            ext.at[pl.ds(urows, HALO)], ext.at[pl.ds(0, HALO)], halo_ss.at[1], halo_rs.at[1], *up
        ).wait_recv()

    @pl.when(has_up)
    def _():
        halo_up.wait_send()

    @pl.when(has_down)
    def _():
        halo_down.wait_send()

    state = ext[...]
    forcing = []
    for t in range(STEPS):
        state = (
            coef[4] * state
            + coef[0] * pltpu.roll(state, erows - 1, 0)
            + coef[1] * pltpu.roll(state, 1, 0)
            + coef[2] * pltpu.roll(state, flon - 1, 1)
            + coef[3] * pltpu.roll(state, 1, 1)
        )
        wts[t] = wts[t] * (state - vals[t])
    adjoint = None
    for t in reversed(range(STEPS)):
        adjoint = wts[t] if adjoint is None else adjoint + wts[t]
        adjoint = (
            coef[4] * adjoint
            + pltpu.roll(coef[1] * adjoint, erows - 1, 0)
            + pltpu.roll(coef[0] * adjoint, 1, 0)
            + pltpu.roll(coef[3] * adjoint, flon - 1, 1)
            + pltpu.roll(coef[2] * adjoint, 1, 1)
        )
    adjg[me] = adjoint[HALO : HALO + urows]

    def adj_copy(p):
        return send(adjg.at[me], adjg.at[me], adj_ss.at[p], adj_rs.at[pair], 2 * p + core, z)

    def adj_arrival(p):
        unit = 2 * p + core
        return send(adjg.at[unit], adjg.at[unit], adj_ss.at[p], adj_rs.at[p], unit, z)

    def relay(p):
        unit = 2 * p + core
        return send(adjg.at[unit], adjg.at[unit], rel_ss.at[p], rel_rs.at[p], partner, z)

    def relay_arrival(p):
        unit = 2 * p + (1 - core)
        return send(adjg.at[unit], adjg.at[unit], rel_ss.at[p], rel_rs.at[p], partner, z)

    for i in range(1, npairs):
        adj_copy((pair + i) % npairs).start()

    directions = ((0, 1), (1, -1))

    def g_target(way, step, k, there, level):
        if k >= 3:
            return z + step, relayed.at[way, there, level], relayed_rs.at[way, there, level]
        slot = 2 * way + k - 1
        return there, gr.at[slot, level], g_rs.at[slot, level]

    def g_copy(way, step, k, level):
        there = z + step * k
        lat, dst, arrived = g_target(way, step, k, there, level)
        return send(gb.at[there, level], dst, g_ss.at[there, level], arrived, me, lat)

    def exists(place):
        return (place >= 0) & (place < nlat)

    def g_first(level):
        for k in range(nlat - 1, 0, -1):
            for way, step in directions:
                ready = exists(z + step * k)
                if k > 1:
                    ready = ready & jnp.logical_not(exists(z - step))

                @pl.when(ready)
                def _():
                    g_copy(way, step, k, level).start()

    def g_later(level):
        for k in range(nlat - 2, 1, -1):
            for way, step in directions:
                there = z + step * k

                @pl.when(exists(there) & exists(z - step))
                def _():
                    send(
                        gb.at[there, level],
                        relayed.at[way, there, level],
                        g_ss.at[there, level],
                        relayed_rs.at[way, there, level],
                        me,
                        z - step,
                    ).wait_recv()
                    gb[there, level] = gb[there, level] + relayed[way, there, level]
                    g_copy(way, step, k, level).start()

    def backward(level):
        field = adjg[pl.ds(level * groups, groups)].reshape(rows, flon)
        product = jnp.concatenate(
            [pert_ref[m, level].astype(F32) * field for m in range(members)], axis=0
        )
        hi, lo = split2(product)
        projected = dot(jnp.concatenate([hi, lo], axis=0), lon_t[...])
        projected = projected[: members * rows] + projected[members * rows :]
        projected = jnp.concatenate(
            [projected[m * rows : (m + 1) * rows] for m in range(members)], axis=1
        )
        hi, lo = split2(projected)
        banded = dot(lat_t2, jnp.concatenate([hi, lo], axis=0))
        gb[:, level] = banded.reshape(nlat, -1, members * clon)
        g_first(level)

    def order(j):
        p = (pair + 2 * npairs - j) % npairs
        if groups == 2:
            return p
        return 2 * p + jnp.where(j < npairs, core, 1 - core)

    def step_back(j):
        backward(order(j))

        @pl.when(j >= LAG)
        def _():
            g_later(order(j - LAG))

    def near(i, carry):
        p = (pair + npairs - i) % npairs

        @pl.when(i > 0)
        def _():
            adj_arrival(p).wait_recv()

        relay(p).start()
        if groups == 1:
            step_back(i)
        return carry

    lax.fori_loop(0, npairs, near, 0)

    def far(i, carry):
        p = (pair + npairs - i) % npairs
        relay_arrival(p).wait_recv()
        step_back(npairs + i if groups == 1 else i)
        return carry

    lax.fori_loop(0, npairs, far, 0)

    def trail(j, carry):
        g_later(order(j))
        return carry

    lax.fori_loop(lev - LAG, lev, trail, 0)

    for i in range(1, nmem):
        inc_arrival((me + nmem - i) % nmem).wait_recv()
    inc_ref[...] = incr[...].reshape(lev * rows, cols)

    def finish(j, carry):
        level = order(j)
        for k in range(1, min(3, nlat)):
            for way, step in directions:
                source = z - step * k
                slot = 2 * way + k - 1

                @pl.when(exists(source))
                def _():
                    send(
                        gb.at[z, level],
                        gr.at[slot, level],
                        g_ss.at[z, level],
                        g_rs.at[slot, level],
                        me,
                        source,
                    ).wait_recv()
                    gb[z, level] = gb[z, level] + gr[slot, level]

        return carry

    lax.fori_loop(0, lev, finish, 0)
    for m in range(members):
        total = jnp.swapaxes(gb[z, :, :, m * clon : (m + 1) * clon], 0, 1)
        total = total * scale
        for c in range(total.shape[0]):
            at = (c * members + m) * lev
            grad_ref[at : at + lev] = total[c]

    for i in range(1, nmem):
        aux_copy((me + i) % nmem).wait_send()
        inc_copy((me + i) % nmem).wait_send()
    for p in range(npairs):
        pr_copy(p).wait_send()
        relay(p).wait_send()
    for i in range(1, npairs):
        rs_copy((pair + i) % npairs).wait_send()
        adj_copy((pair + i) % npairs).wait_send()

    def drain(level, carry):
        for i in range(1, nlat):
            there = (z + i) % nlat
            cg_copy(there, level).wait_send()
            send(
                gb.at[there, level],
                gr.at[0, level],
                g_ss.at[there, level],
                g_rs.at[0, level],
                me,
                there,
            ).wait_send()
        return carry

    lax.fori_loop(0, lev, drain, 0)


def finish_kernel(banded_ref, coarse_ref, tiles_ref, grad_ref, inc_ref):
    grad_ref[...] = banded_ref[...] + coarse_ref[...].astype(F32)
    inc_ref[...] = tiles_ref[...]


def body(
    nmem,
    nlat,
    coarse_weights,
    perturbations,
    lat_matrix,
    lon_matrix,
    wind_field,
    observed_cell,
    observed_value,
    observed_weight,
):
    members, lev, rows, flon = perturbations.shape
    cband, _, _, clon = coarse_weights.shape
    cols = wind_field.shape[2]
    blocks = cols // OBLK
    groups = nmem // lev
    urows = rows // groups
    erows = urows + 2 * HALO
    npairs = nmem // 2
    assert nmem == lev * groups and nmem % 2 == 0 and groups <= 2 and urows % 8 == 0 and urows >= HALO
    assert 2 * cols == LANES and 3 * STEPS * blocks <= LANES
    vmem = pl.BlockSpec(memory_space=pltpu.VMEM)
    dma = pltpu.SemaphoreType.DMA
    width = members * clon
    arguments = (
        coarse_weights,
        perturbations,
        lat_matrix,
        lon_matrix,
        wind_field,
        jnp.swapaxes(observed_cell, 2, 3),
        jnp.swapaxes(observed_value, 2, 3),
        jnp.swapaxes(observed_weight, 2, 3),
    )
    banded, increment = pl.pallas_call(
        functools.partial(kernel, nmem, nlat, float(1.0 / (members * nmem - 1) ** 0.5)),
        out_shape=(
            jax.ShapeDtypeStruct((cband * members * lev, clon), F32),
            jax.ShapeDtypeStruct((lev * rows, cols), F32),
        ),
        in_specs=[pl.BlockSpec(memory_space=pltpu.HBM)] * len(arguments),
        out_specs=(vmem, vmem),
        scratch_shapes=[
            *[pltpu.VMEM(x.shape, x.dtype) for x in arguments],
            pltpu.VMEM((lev, rows, 2 * LANES), F32),
            pltpu.VMEM((nlat, lev, members, cband, clon), BF16),
            pltpu.VMEM((nmem, erows, 2 * LANES), F32),
            pltpu.VMEM((nmem, urows, flon), F32),
            pltpu.VMEM((npairs, urows, flon), F32),
            pltpu.VMEM((npairs, urows, flon), F32),
            pltpu.VMEM((erows, flon), F32),
            pltpu.VMEM((2 * LANES, 3 * STEPS * LANES), BF16),
            pltpu.VMEM((5, erows, flon), F32),
            pltpu.VMEM((STEPS, erows, flon), F32),
            pltpu.VMEM((STEPS, erows, flon), F32),
            pltpu.VMEM((nmem, urows, cols), F32),
            pltpu.VMEM((lev, rows, cols), F32),
            pltpu.VMEM((nmem, urows, flon), F32),
            pltpu.VMEM((nlat, lev, cband, width), F32),
            pltpu.VMEM((4, lev, cband, width), F32),
            pltpu.VMEM((2, nlat, lev, cband, width), F32),
            pltpu.VMEM((flon, clon), BF16),
            dma((len(arguments),)),
            dma((nlat, lev)),
            dma((nlat, lev)),
            dma((nmem,)),
            dma((nmem,)),
            dma((2,)),
            dma((2,)),
            dma((npairs,)),
            dma((npairs,)),
            dma((npairs,)),
            dma((npairs,)),
            dma((2,)),
            dma((2,)),
            dma((nmem,)),
            dma((nmem,)),
            dma((npairs,)),
            dma((npairs,)),
            dma((npairs,)),
            dma((npairs,)),
            dma((nlat, lev)),
            dma((4, lev)),
            dma((2, nlat, lev)),
        ],
        compiler_params=pltpu.CompilerParams(
            collective_id=0, has_side_effects=True, vmem_limit_bytes=60 * 1024 * 1024
        ),
    )(*arguments)
    gradient, increment = pl.pallas_call(
        finish_kernel,
        out_shape=(
            jax.ShapeDtypeStruct((cband * members * lev, clon), F32),
            jax.ShapeDtypeStruct((lev * rows, cols), F32),
        ),
        in_specs=[vmem] * 3,
        out_specs=(vmem, vmem),
    )(banded, coarse_weights.reshape(-1, clon), increment)
    return gradient.reshape(coarse_weights.shape), increment.reshape(lev, rows, cols)


def solution(mesh):
    in_specs = (
        P("lat", "mem", None, None),
        P("mem", None, "lat", None),
        P("lat", None),
        P(),
        P(None, "lat", "mem"),
        P(None, None, "lat", "mem"),
        P(None, None, "lat", "mem"),
        P(None, None, "lat", "mem"),
    )
    out_specs = (P("lat", "mem", None, None), P(None, "lat", "mem"))
    call = functools.partial(body, mesh.shape["mem"], mesh.shape["lat"])
    return jax.shard_map(call, mesh=mesh, in_specs=in_specs, out_specs=out_specs, check_vma=False)
```

```python
import functools

import jax
import jax.numpy as jnp
from jax import lax
from jax.experimental import pallas as pl
from jax.experimental.pallas import tpu as pltpu
from jax.sharding import PartitionSpec as P

STEPS = 4
OBLK = 8
HALO = 2 * STEPS
LAG = 3
LANES = 128
DIFFUSION = 0.2
F32 = jnp.float32
BF16 = jnp.bfloat16


def split2(x):
    hi = x.astype(BF16)
    return hi, (x - hi.astype(F32)).astype(BF16)


def dot(a, b, dims=((1,), (0,))):
    return lax.dot_general(a, b, (dims, ((), ())), preferred_element_type=F32)


def kernel(
    nmem,
    nlat,
    scale,
    coarse_hbm,
    pert_hbm,
    lat_hbm,
    lon_hbm,
    wind_hbm,
    cell_hbm,
    value_hbm,
    weight_hbm,
    grad_ref,
    inc_ref,
    coarse_ref,
    pert_ref,
    lat_ref,
    lon_ref,
    wind_ref,
    cell_ref,
    value_ref,
    weight_ref,
    aux_ref,
    cg,
    auxg,
    part,
    pr,
    rs,
    ext,
    spread,
    coef,
    wts,
    vals,
    itile,
    incr,
    adjg,
    gb,
    gr,
    relayed,
    lon_t,
    in_sem,
    cg_ss,
    cg_rs,
    aux_ss,
    aux_rs,
    ah_ss,
    ah_rs,
    pr_ss,
    pr_rs,
    rs_ss,
    rs_rs,
    halo_ss,
    halo_rs,
    inc_ss,
    inc_rs,
    adj_ss,
    adj_rs,
    rel_ss,
    rel_rs,
    g_ss,
    g_rs,
    relayed_rs,
):
    members, lev, rows, flon = pert_ref.shape
    clon = lon_ref.shape[0]
    cols = flon // nmem
    groups = nmem // lev
    urows = rows // groups
    erows = urows + 2 * HALO
    npairs = nmem // 2
    me = lax.axis_index("mem")
    z = lax.axis_index("lat")
    pair = me // 2
    core = me % 2
    partner = pair * 2 + (1 - core)
    my_level = me // groups
    my_group = me % groups
    my_row = my_group * urows
    block = z * groups + my_group
    has_up = block > 0
    has_down = block < nlat * groups - 1

    def neighbour(shift):
        there = block + shift
        return (my_level * groups + (there + groups) % groups, (there + groups) // groups - 1)

    up = neighbour(-1)
    down = neighbour(1)

    def send(src, dst, ss, rsem, mem, lat):
        return pltpu.make_async_remote_copy(
            src_ref=src,
            dst_ref=dst,
            send_sem=ss,
            recv_sem=rsem,
            device_id={"mem": mem, "lat": lat},
            device_id_type=pl.DeviceIdType.MESH,
        )

    arguments = (
        (coarse_hbm, coarse_ref),
        (lat_hbm, lat_ref),
        (lon_hbm, lon_ref),
        (wind_hbm, wind_ref),
        (cell_hbm, cell_ref),
        (value_hbm, value_ref),
        (weight_hbm, weight_ref),
        (pert_hbm, pert_ref),
    )
    loads = [
        pltpu.make_async_copy(src, dst, in_sem.at[i]) for i, (src, dst) in enumerate(arguments)
    ]
    for load in loads:
        load.start()

    barrier = pltpu.get_barrier_semaphore()

    def greet(mem, lat):
        pl.semaphore_signal(
            barrier, inc=1, device_id={"mem": mem, "lat": lat}, device_id_type=pl.DeviceIdType.MESH
        )

    for i in range(1, nlat):
        greet(me, (z + i) % nlat)
    for i in range(1, nmem):
        greet((me + i) % nmem, z)
    loads[0].wait()
    for m in range(members):
        mine = jnp.swapaxes(coarse_ref[:, m].astype(F32), 0, 1).astype(BF16)
        for level in range(lev):
            cg[z, level, m] = mine[level]
    pl.semaphore_wait(barrier, nmem + nlat - 2)
    if groups > 1:
        far_up = has_up & (my_group == 0)
        far_down = has_down & (my_group == groups - 1)

        @pl.when(far_up)
        def _():
            greet(*up)

        @pl.when(far_down)
        def _():
            greet(*down)

        @pl.when(far_up)
        def _():
            pl.semaphore_wait(barrier, 1)

        @pl.when(far_down)
        def _():
            pl.semaphore_wait(barrier, 1)

    def level_at(i):
        if groups > 1:
            return i
        half = lev // 2
        p = (pair + 1 + i) % npairs
        return 2 * p + jnp.where(i < half, 1 - core, core)

    def cg_copy(there, level):
        return send(
            cg.at[z, level], cg.at[z, level], cg_ss.at[there, level], cg_rs.at[z, level], me, there
        )

    def cg_arrival(source, level):
        return send(
            cg.at[source, level],
            cg.at[source, level],
            cg_ss.at[source, level],
            cg_rs.at[source, level],
            me,
            source,
        )

    def spread_coarse(i, carry):
        for j in range(1, nlat):
            cg_copy((z + j) % nlat, level_at(i)).start()
        return carry

    lax.fori_loop(0, lev, spread_coarse, 0)

    for load in loads[1:-1]:
        load.wait()

    blank = jnp.zeros((LANES - 3 * STEPS * (cols // OBLK), rows), F32)
    winds = jnp.concatenate([wind_ref[0], wind_ref[1]], axis=1)

    def pack(level, carry):
        pieces = [ref[t, level] for ref in (weight_ref, value_ref) for t in range(STEPS)]
        pieces += [cell_ref[t, level].astype(F32) for t in range(STEPS)]
        aux_ref[level, :, :LANES] = jnp.transpose(jnp.concatenate(pieces + [blank], axis=0))
        aux_ref[level, :, LANES:] = winds
        return carry

    lax.fori_loop(0, lev, pack, 0)

    def aux_copy(there):
        return send(
            aux_ref.at[there // groups, pl.ds(pl.multiple_of((there % groups) * urows, 8), urows)],
            auxg.at[me, pl.ds(HALO, urows)],
            aux_ss.at[there],
            aux_rs.at[me],
            there,
            z,
        )

    def aux_arrival(source):
        return send(
            aux_ref.at[0, pl.ds(0, urows)],
            auxg.at[source, pl.ds(HALO, urows)],
            aux_ss.at[source],
            aux_rs.at[source],
            source,
            z,
        )

    for i in range(1, nmem):
        aux_copy((me + i) % nmem).start()

    auxg[me, HALO : HALO + urows] = aux_ref[my_level, pl.ds(pl.multiple_of(my_row, 8), urows)]

    @pl.when(jnp.logical_not(has_up))
    def _():
        auxg[:, :HALO] = jnp.zeros((nmem, HALO, 2 * LANES), F32)
        ext[:HALO] = jnp.zeros((HALO, flon), F32)

    @pl.when(jnp.logical_not(has_down))
    def _():
        auxg[:, HALO + urows :] = jnp.zeros((nmem, HALO, 2 * LANES), F32)
        ext[HALO + urows :] = jnp.zeros((HALO, flon), F32)

    per_tile = cols // OBLK
    k = lax.broadcasted_iota(jnp.int32, (2 * LANES, LANES), 0)
    n = lax.broadcasted_iota(jnp.int32, (2 * LANES, LANES), 1)
    for piece in range(3 * STEPS):
        hit = k == (n // cols) * LANES + piece * per_tile + (n % cols) // OBLK
        spread[:, piece * LANES : (piece + 1) * LANES] = jnp.where(hit, 1.0, 0.0).astype(BF16)

    lat_f32 = lat_ref[...].astype(F32)
    lat_bf = lat_ref[...]
    lat_t = jnp.transpose(lat_f32).astype(BF16)
    lat_t2 = jnp.concatenate([lat_t, lat_t], axis=1)
    lon = lon_ref[...]
    lon_t[...] = jnp.transpose(lon.astype(F32)).astype(BF16)

    loads[-1].wait()

    def pr_copy(p):
        unit = 2 * p + (1 - core)
        return send(part.at[unit], pr.at[p], pr_ss.at[p], pr_rs.at[p], partner, z)

    def pr_arrival(p):
        return send(part.at[2 * p + core], pr.at[p], pr_ss.at[p], pr_rs.at[p], partner, z)

    def rs_copy(p):
        return send(pr.at[p], rs.at[pair], rs_ss.at[p], rs_rs.at[pair], 2 * p + core, z)

    def rs_arrival(p):
        return send(pr.at[p], rs.at[p], rs_ss.at[p], rs_rs.at[p], 2 * p + core, z)

    def combine(i, carry):
        p = (pair + 1 + i) % npairs
        pr_arrival(p).wait_recv()
        pr[p] = pr[p] + part[2 * p + core]

        @pl.when(p != pair)
        def _():
            rs_copy(p).start()

        return carry

    ah_up = send(
        auxg.at[:, pl.ds(HALO, HALO)],
        auxg.at[:, pl.ds(HALO + urows, HALO)],
        ah_ss.at[0],
        ah_rs.at[0],
        *up,
    )
    ah_down = send(
        auxg.at[:, pl.ds(urows, HALO)], auxg.at[:, pl.ds(0, HALO)], ah_ss.at[1], ah_rs.at[1], *down
    )


    def exchange_aux():
        for i in range(1, nmem):
            aux_arrival((me + nmem - i) % nmem).wait_recv()

        @pl.when(has_up)
        def _():
            ah_up.start()

        @pl.when(has_down)
        def _():
            ah_down.start()

    def forward(i, carry):
        level = level_at(i)
        for j in range(1, nlat):
            cg_arrival((z + nlat - j) % nlat, level).wait_recv()
        coarse = jnp.concatenate(
            [cg[:, level, m].astype(F32).reshape(-1, clon) for m in range(members)], axis=1
        ).astype(BF16)
        partly = dot(lat_bf, coarse)
        partly = jnp.concatenate(
            [partly[:, m * clon : (m + 1) * clon] for m in range(members)], axis=0
        )
        hi, lo = split2(partly)
        localized = dot(jnp.concatenate([hi, lo], axis=0), lon)
        localized = localized[: members * rows] + localized[members * rows :]
        total = localized[:rows] * pert_ref[0, level].astype(F32)
        for m in range(1, members):
            total += localized[m * rows : (m + 1) * rows] * pert_ref[m, level].astype(F32)
        part[pl.ds(level * groups, groups)] = total.reshape(groups, urows, flon)

        @pl.when(i == lev // 2)
        def _():
            exchange_aux()

        if groups == 1:

            @pl.when(i < lev // 2)
            def _():
                pr_copy((pair + 1 + i) % npairs).start()

            @pl.when(i >= lev // 2)
            def _():
                combine(i - lev // 2, 0)

        else:
            for g in range(groups // 2):
                pr_copy(level * (groups // 2) + g).start()
        return carry

    lax.fori_loop(0, lev, forward, 0)

    if groups > 1:
        lax.fori_loop(0, npairs, combine, 0)

    @pl.when(has_down)
    def _():
        ah_up_arrival = send(
            auxg.at[:, pl.ds(HALO, HALO)],
            auxg.at[:, pl.ds(HALO + urows, HALO)],
            ah_ss.at[0],
            ah_rs.at[0],
            *down,
        )
        ah_up_arrival.wait_recv()

    @pl.when(has_up)
    def _():
        ah_down_arrival = send(
            auxg.at[:, pl.ds(urows, HALO)],
            auxg.at[:, pl.ds(0, HALO)],
            ah_ss.at[1],
            ah_rs.at[1],
            *up,
        )
        ah_down_arrival.wait_recv()

    @pl.when(has_up)
    def _():
        ah_up.wait_send()

    @pl.when(has_down)
    def _():
        ah_down.wait_send()

    place = block * urows - HALO + lax.broadcasted_iota(jnp.int32, (erows, LANES), 0)
    inside = (place >= 0) & (place < nlat * rows)
    lane = lax.broadcasted_iota(jnp.int32, (erows, LANES), 1)
    tiles = LANES // cols
    for q in range(flon // LANES):
        first, second = auxg[tiles * q], auxg[tiles * q + 1]
        lhs = jnp.concatenate([first[:, :LANES], second[:, :LANES]], axis=1)
        hi, rest = lhs.astype(BF16), lhs
        rest = rest - hi.astype(F32)
        mid, low = split2(rest)
        out = dot(jnp.concatenate([hi, mid, low], axis=0), spread[...])
        out = out[:erows] + out[erows : 2 * erows] + out[2 * erows :]
        at = slice(q * LANES, (q + 1) * LANES)
        for t in range(STEPS):
            weight = out[:, t * LANES : (t + 1) * LANES]
            value = out[:, (STEPS + t) * LANES : (STEPS + t + 1) * LANES]
            cell = out[:, (2 * STEPS + t) * LANES : (2 * STEPS + t + 1) * LANES]
            hit = cell == (lane % OBLK).astype(F32)
            wts[t, :, at] = jnp.where(hit, weight, 0.0)
            vals[t, :, at] = value
        w0, w1 = first[:, LANES:], second[:, LANES:]
        lower = lane < cols
        c0 = jnp.where(lower, w0, pltpu.roll(w1, cols, 1))
        c1 = jnp.where(lower, pltpu.roll(w0, cols, 1), w1)
        east_in = inside & (lane + q * LANES < flon - 1)
        west_in = inside & (lane + q * LANES > 0)
        coef[0, :, at] = jnp.where(inside, DIFFUSION - 0.5 * c1, 0.0)
        coef[1, :, at] = jnp.where(inside, DIFFUSION + 0.5 * c1, 0.0)
        coef[2, :, at] = jnp.where(east_in, DIFFUSION - 0.5 * c0, 0.0)
        coef[3, :, at] = jnp.where(west_in, DIFFUSION + 0.5 * c0, 0.0)
        coef[4, :, at] = jnp.where(inside, jnp.full((erows, LANES), 1.0 - 4.0 * DIFFUSION, F32), 0.0)

    total = pr[pair]
    for i in range(1, npairs):
        p = (pair + npairs - i) % npairs
        rs_arrival(p).wait_recv()
        total = total + rs[p]
    total = total * scale
    ext[HALO : HALO + urows] = total
    halo_up = send(
        ext.at[pl.ds(HALO, HALO)],
        ext.at[pl.ds(HALO + urows, HALO)],
        halo_ss.at[0],
        halo_rs.at[0],
        *up,
    )
    halo_down = send(
        ext.at[pl.ds(urows, HALO)], ext.at[pl.ds(0, HALO)], halo_ss.at[1], halo_rs.at[1], *down
    )

    @pl.when(has_up)
    def _():
        halo_up.start()

    @pl.when(has_down)
    def _():
        halo_down.start()

    for m in range(nmem):
        itile[m] = total[:, m * cols : (m + 1) * cols]

    def inc_copy(there):
        return send(
            itile.at[there],
            incr.at[my_level, pl.ds(pl.multiple_of(my_row, 8), urows)],
            inc_ss.at[there],
            inc_rs.at[me],
            there,
            z,
        )

    def inc_arrival(source):
        return send(
            itile.at[source],
            incr.at[
                source // groups, pl.ds(pl.multiple_of((source % groups) * urows, 8), urows)
            ],
            inc_ss.at[source],
            inc_rs.at[source],
            source,
            z,
        )

    for i in range(1, nmem):
        inc_copy((me + i) % nmem).start()
    incr[my_level, pl.ds(pl.multiple_of(my_row, 8), urows)] = itile[me]

    @pl.when(has_down)
    def _():
        send(
            ext.at[pl.ds(HALO, HALO)],
            ext.at[pl.ds(HALO + urows, HALO)],
            halo_ss.at[0],
            halo_rs.at[0],
            *down,
        ).wait_recv()

    @pl.when(has_up)
    def _():
        send(
            ext.at[pl.ds(urows, HALO)], ext.at[pl.ds(0, HALO)], halo_ss.at[1], halo_rs.at[1], *up
        ).wait_recv()

    @pl.when(has_up)
    def _():
        halo_up.wait_send()

    @pl.when(has_down)
    def _():
        halo_down.wait_send()

    state = ext[...]
    forcing = []
    for t in range(STEPS):
        state = (
            coef[4] * state
            + coef[0] * pltpu.roll(state, erows - 1, 0)
            + coef[1] * pltpu.roll(state, 1, 0)
            + coef[2] * pltpu.roll(state, flon - 1, 1)
            + coef[3] * pltpu.roll(state, 1, 1)
        )
        wts[t] = wts[t] * (state - vals[t])
    adjoint = None
    for t in reversed(range(STEPS)):
        adjoint = wts[t] if adjoint is None else adjoint + wts[t]
        adjoint = (
            coef[4] * adjoint
            + pltpu.roll(coef[1] * adjoint, erows - 1, 0)
            + pltpu.roll(coef[0] * adjoint, 1, 0)
            + pltpu.roll(coef[3] * adjoint, flon - 1, 1)
            + pltpu.roll(coef[2] * adjoint, 1, 1)
        )
    adjg[me] = adjoint[HALO : HALO + urows]

    def adj_copy(p):
        return send(adjg.at[me], adjg.at[me], adj_ss.at[p], adj_rs.at[pair], 2 * p + core, z)

    def adj_arrival(p):
        unit = 2 * p + core
        return send(adjg.at[unit], adjg.at[unit], adj_ss.at[p], adj_rs.at[p], unit, z)

    def relay(p):
        unit = 2 * p + core
        return send(adjg.at[unit], adjg.at[unit], rel_ss.at[p], rel_rs.at[p], partner, z)

    def relay_arrival(p):
        unit = 2 * p + (1 - core)
        return send(adjg.at[unit], adjg.at[unit], rel_ss.at[p], rel_rs.at[p], partner, z)

    for i in range(1, npairs):
        adj_copy((pair + i) % npairs).start()

    directions = ((0, 1), (1, -1))

    def g_target(way, step, k, there, level):
        if k >= 3:
            return z + step, relayed.at[way, there, level], relayed_rs.at[way, there, level]
        slot = 2 * way + k - 1
        return there, gr.at[slot, level], g_rs.at[slot, level]

    def g_copy(way, step, k, level):
        there = z + step * k
        lat, dst, arrived = g_target(way, step, k, there, level)
        return send(gb.at[there, level], dst, g_ss.at[there, level], arrived, me, lat)

    def exists(place):
        return (place >= 0) & (place < nlat)

    def g_first(level):
        for k in range(nlat - 1, 0, -1):
            for way, step in directions:
                ready = exists(z + step * k)
                if k > 1:
                    ready = ready & jnp.logical_not(exists(z - step))

                @pl.when(ready)
                def _():
                    g_copy(way, step, k, level).start()

    def g_later(level):
        for k in range(nlat - 2, 1, -1):
            for way, step in directions:
                there = z + step * k

                @pl.when(exists(there) & exists(z - step))
                def _():
                    send(
                        gb.at[there, level],
                        relayed.at[way, there, level],
                        g_ss.at[there, level],
                        relayed_rs.at[way, there, level],
                        me,
                        z - step,
                    ).wait_recv()
                    gb[there, level] = gb[there, level] + relayed[way, there, level]
                    g_copy(way, step, k, level).start()

    def backward(level):
        field = adjg[pl.ds(level * groups, groups)].reshape(rows, flon)
        product = jnp.concatenate(
            [pert_ref[m, level].astype(F32) * field for m in range(members)], axis=0
        )
        hi, lo = split2(product)
        projected = dot(jnp.concatenate([hi, lo], axis=0), lon_t[...])
        projected = projected[: members * rows] + projected[members * rows :]
        projected = jnp.concatenate(
            [projected[m * rows : (m + 1) * rows] for m in range(members)], axis=1
        )
        hi, lo = split2(projected)
        banded = dot(lat_t2, jnp.concatenate([hi, lo], axis=0))
        gb[:, level] = banded.reshape(nlat, -1, members * clon)
        g_first(level)

    def order(j):
        if groups == 2:
            return (pair + npairs - j) % npairs
        near_turn = (j == 0) | ((j >= 2) & (j <= npairs))
        i = jnp.where(j < 2, 0, jnp.where(near_turn, j - 1, j - npairs))
        return 2 * ((pair + npairs - i) % npairs) + jnp.where(near_turn, core, 1 - core)

    def step_back(j):
        backward(order(j))

        @pl.when(j >= LAG)
        def _():
            g_later(order(j - LAG))

    def near(i, carry):
        p = (pair + npairs - i) % npairs

        @pl.when(i > 0)
        def _():
            adj_arrival(p).wait_recv()

        relay(p).start()
        if groups == 1:
            step_back(jnp.where(i == 0, 0, i + 1))
        return carry


    def far(i, carry):
        p = (pair + npairs - i) % npairs
        relay_arrival(p).wait_recv()
        step_back(jnp.where(i == 0, 1, npairs + i) if groups == 1 else i)
        return carry

    for first, last in ((0, 1), (1, npairs)):
        lax.fori_loop(first, last, near, 0)
        lax.fori_loop(first, last, far, 0)

    def trail(j, carry):
        g_later(order(j))
        return carry

    lax.fori_loop(lev - LAG, lev, trail, 0)

    for i in range(1, nmem):
        inc_arrival((me + nmem - i) % nmem).wait_recv()
    inc_ref[...] = incr[...].reshape(lev * rows, cols)

    def finish(j, carry):
        level = order(j)
        for k in range(1, min(3, nlat)):
            for way, step in directions:
                source = z - step * k
                slot = 2 * way + k - 1

                @pl.when(exists(source))
                def _():
                    send(
                        gb.at[z, level],
                        gr.at[slot, level],
                        g_ss.at[z, level],
                        g_rs.at[slot, level],
                        me,
                        source,
                    ).wait_recv()
                    gb[z, level] = gb[z, level] + gr[slot, level]

        return carry

    lax.fori_loop(0, lev, finish, 0)
    for m in range(members):
        total = jnp.swapaxes(gb[z, :, :, m * clon : (m + 1) * clon], 0, 1)
        total = total * scale
        for c in range(total.shape[0]):
            at = (c * members + m) * lev
            grad_ref[at : at + lev] = total[c]

    for i in range(1, nmem):
        aux_copy((me + i) % nmem).wait_send()
        inc_copy((me + i) % nmem).wait_send()
    for p in range(npairs):
        pr_copy(p).wait_send()
        relay(p).wait_send()
    for i in range(1, npairs):
        rs_copy((pair + i) % npairs).wait_send()
        adj_copy((pair + i) % npairs).wait_send()

    def drain(level, carry):
        for i in range(1, nlat):
            there = (z + i) % nlat
            cg_copy(there, level).wait_send()
            send(
                gb.at[there, level],
                gr.at[0, level],
                g_ss.at[there, level],
                g_rs.at[0, level],
                me,
                there,
            ).wait_send()
        return carry

    lax.fori_loop(0, lev, drain, 0)


def finish_kernel(banded_ref, coarse_ref, tiles_ref, grad_ref, inc_ref):
    grad_ref[...] = banded_ref[...] + coarse_ref[...].astype(F32)
    inc_ref[...] = tiles_ref[...]


def body(
    nmem,
    nlat,
    coarse_weights,
    perturbations,
    lat_matrix,
    lon_matrix,
    wind_field,
    observed_cell,
    observed_value,
    observed_weight,
):
    members, lev, rows, flon = perturbations.shape
    cband, _, _, clon = coarse_weights.shape
    cols = wind_field.shape[2]
    blocks = cols // OBLK
    groups = nmem // lev
    urows = rows // groups
    erows = urows + 2 * HALO
    npairs = nmem // 2
    assert nmem == lev * groups and nmem % 2 == 0 and groups <= 2 and urows % 8 == 0 and urows >= HALO
    assert 2 * cols == LANES and 3 * STEPS * blocks <= LANES
    vmem = pl.BlockSpec(memory_space=pltpu.VMEM)
    dma = pltpu.SemaphoreType.DMA
    width = members * clon
    arguments = (
        coarse_weights,
        perturbations,
        lat_matrix,
        lon_matrix,
        wind_field,
        jnp.swapaxes(observed_cell, 2, 3),
        jnp.swapaxes(observed_value, 2, 3),
        jnp.swapaxes(observed_weight, 2, 3),
    )
    banded, increment = pl.pallas_call(
        functools.partial(kernel, nmem, nlat, float(1.0 / (members * nmem - 1) ** 0.5)),
        out_shape=(
            jax.ShapeDtypeStruct((cband * members * lev, clon), F32),
            jax.ShapeDtypeStruct((lev * rows, cols), F32),
        ),
        in_specs=[pl.BlockSpec(memory_space=pltpu.HBM)] * len(arguments),
        out_specs=(vmem, vmem),
        scratch_shapes=[
            *[pltpu.VMEM(x.shape, x.dtype) for x in arguments],
            pltpu.VMEM((lev, rows, 2 * LANES), F32),
            pltpu.VMEM((nlat, lev, members, cband, clon), BF16),
            pltpu.VMEM((nmem, erows, 2 * LANES), F32),
            pltpu.VMEM((nmem, urows, flon), F32),
            pltpu.VMEM((npairs, urows, flon), F32),
            pltpu.VMEM((npairs, urows, flon), F32),
            pltpu.VMEM((erows, flon), F32),
            pltpu.VMEM((2 * LANES, 3 * STEPS * LANES), BF16),
            pltpu.VMEM((5, erows, flon), F32),
            pltpu.VMEM((STEPS, erows, flon), F32),
            pltpu.VMEM((STEPS, erows, flon), F32),
            pltpu.VMEM((nmem, urows, cols), F32),
            pltpu.VMEM((lev, rows, cols), F32),
            pltpu.VMEM((nmem, urows, flon), F32),
            pltpu.VMEM((nlat, lev, cband, width), F32),
            pltpu.VMEM((4, lev, cband, width), F32),
            pltpu.VMEM((2, nlat, lev, cband, width), F32),
            pltpu.VMEM((flon, clon), BF16),
            dma((len(arguments),)),
            dma((nlat, lev)),
            dma((nlat, lev)),
            dma((nmem,)),
            dma((nmem,)),
            dma((2,)),
            dma((2,)),
            dma((npairs,)),
            dma((npairs,)),
            dma((npairs,)),
            dma((npairs,)),
            dma((2,)),
            dma((2,)),
            dma((nmem,)),
            dma((nmem,)),
            dma((npairs,)),
            dma((npairs,)),
            dma((npairs,)),
            dma((npairs,)),
            dma((nlat, lev)),
            dma((4, lev)),
            dma((2, nlat, lev)),
        ],
        compiler_params=pltpu.CompilerParams(
            collective_id=0, has_side_effects=True, vmem_limit_bytes=60 * 1024 * 1024
        ),
    )(*arguments)
    gradient, increment = pl.pallas_call(
        finish_kernel,
        out_shape=(
            jax.ShapeDtypeStruct((cband * members * lev, clon), F32),
            jax.ShapeDtypeStruct((lev * rows, cols), F32),
        ),
        in_specs=[vmem] * 3,
        out_specs=(vmem, vmem),
    )(banded, coarse_weights.reshape(-1, clon), increment)
    return gradient.reshape(coarse_weights.shape), increment.reshape(lev, rows, cols)


def solution(mesh):
    in_specs = (
        P("lat", "mem", None, None),
        P("mem", None, "lat", None),
        P("lat", None),
        P(),
        P(None, "lat", "mem"),
        P(None, None, "lat", "mem"),
        P(None, None, "lat", "mem"),
        P(None, None, "lat", "mem"),
    )
    out_specs = (P("lat", "mem", None, None), P(None, "lat", "mem"))
    call = functools.partial(body, mesh.shape["mem"], mesh.shape["lat"])
    return jax.shard_map(call, mesh=mesh, in_specs=in_specs, out_specs=out_specs, check_vma=False)
```
